256 devices in a mesh: seq: 32 (over y_hi, z, core), fsdp: 8 (over y_lo, x).
Axes of the slice: x: 4, y: 4 (y_hi: 2, y_lo: 2; y = y_hi * 2 + y_lo), z: 8, core: 2. Of those that a mesh axis runs over, the one named last changes fastest.
Arguments:
- cotangent: bfloat16 [4096, 1536], P('seq', 'fsdp'), may hold values from -6 to 6
- out_weight: bfloat16 [1536, 1536], P('fsdp', 'seq'), may hold values from -0.15625 to 0.15625
- values: bfloat16 [4096, 1536], P('seq', 'fsdp'), may hold values from -1.5 to 1.5
- gate_input: bfloat16 [4096, 1536], P('seq', 'fsdp'), may hold values from -6 to 6
- conv_out: bfloat16 [4096, 1536], P('seq', 'fsdp'), may hold values from -6 to 6
- filter_taps: bfloat16 [1536, 4096], P('fsdp'), may hold values from -0.09375 to 0.09375
Outputs:
- grad_value: bfloat16 [4096, 1536], P('seq', 'fsdp')
- grad_gate: bfloat16 [4096, 1536], P('seq', 'fsdp')
- grad_filter: float32 [4096, 1536], P('seq', 'fsdp')
- grad_weight: float32 [1536, 1536], P('fsdp', 'seq')
The draws below stay inside these ranges and needn't reach their ends.
All inputs are finite; a program needn't handle non-finite values.
Results may differ from the reference program's by a relative error of at most 0.007.
Values may be sent and summed in bfloat16 or wider, within the bound.
No kernel may reach another device: no remote copies, remote signals or barrier semaphores. Data moves between devices by JAX's collectives and lax.ppermute only.
A program may use at most 128 MiB of HBM per device.

```python
import jax
import jax.numpy as jnp
from jax import lax

D = 1536
TOK_DEV = 128
SEQ = 4096


def raised(drawn, key, source, target, parts, factor):
    def block_of(dim):
        return (jnp.arange(drawn.shape[dim]) // (drawn.shape[dim] // parts)).reshape((-1,) + (1,) * (drawn.ndim - 1 - dim))

    one_side = jax.random.permutation(key, parts)[block_of(target)]
    far = (block_of(target) + parts // 2) % parts
    return jnp.where((block_of(source) == one_side) | (block_of(source) == far), factor * drawn, drawn)


def block_scale(stream_key, dims, shards, least, high):
    def one(axis_at, blocks):
        steps = jax.random.uniform(jax.random.fold_in(jax.random.fold_in(stream_key, 6), axis_at), (blocks,), jnp.float32, least / len(shards), high / len(shards))
        return jnp.repeat(jnp.exp(steps), dims[axis_at] // blocks).reshape((-1,) + (1,) * (len(dims) - axis_at - 1))

    loudness = one(*shards[0])
    for cut in shards[1:]:
        loudness = loudness * one(*cut)
    return loudness


def scatter_about(stream_key, extent, scale, reach, cuts=(), kind=jnp.bfloat16):
    entries = jax.random.normal(stream_key, extent, jnp.float32) * scale
    if len(cuts) > 0:
        entries = block_scale(stream_key, extent, cuts, -0.22, 0.18) * entries
    return jnp.clip(entries, min=-reach, max=reach).astype(kind)


def heavy_noise(own_key, extent, spread, limit, cuts, heavy, kind=jnp.bfloat16):
    values = spread * jax.random.normal(own_key, extent, jnp.float32)
    if cuts:
        values = values * block_scale(own_key, extent, cuts, -0.22, 0.18)
    return jnp.clip(raised(values, jax.random.fold_in(own_key, 3), *heavy), -limit, limit).astype(kind)


def setup_inputs(seed: int = 0) -> dict:
    key_list = jax.random.split(jax.random.key(seed), 7)
    return {
        "cotangent": heavy_noise(key_list[0], (SEQ, D), 1.0, 6.0, ((0, 32), (1, 8)), (0, 1, 32, 2.75)),
        "out_weight": scatter_about(key_list[1], (D, D), D ** -0.5, 0.15625, ((0, 8), (1, 32))),
        "values": scatter_about(key_list[2], (SEQ, D), 0.25, 1.5, ((0, 32), (1, 8))),
        "gate_input": scatter_about(key_list[3], (SEQ, D), 1.0, 6.0, ((0, 32), (1, 8))),
        "conv_out": scatter_about(key_list[4], (SEQ, D), 1.0, 6.0, ((0, 32), (1, 8))),
        "filter_taps": scatter_about(key_list[5], (D, SEQ), SEQ ** -0.5, 0.09375, ((0, 8),)),
    }


def make_tables(block_rows):
    period = 2 * block_rows
    frequency = lax.broadcasted_iota(jnp.int32, (period, period), 0)
    position = lax.broadcasted_iota(jnp.int32, (period, period), 1)
    angles = ((frequency * position) % period).astype(jnp.float32) * (2.0 * jnp.pi / period)
    cosine = jnp.cos(angles)
    sine_part = jnp.sin(angles)
    parity = 1.0 - 2.0 * (position % 2).astype(jnp.float32)
    dft_cos = cosine.astype(jnp.bfloat16)
    dft_sin = (-sine_part).astype(jnp.bfloat16)
    back_cos = (parity * cosine / period).astype(jnp.bfloat16)
    back_sin = (-parity * sine_part / period).astype(jnp.bfloat16)
    return dft_cos, dft_sin, back_cos, back_sin


def high_dot(left, right):
    return jnp.dot(left, right, precision=lax.Precision.HIGHEST, preferred_element_type=jnp.float32)


def round_wide(array):
    narrow = lax.optimization_barrier(array.astype(jnp.bfloat16))
    return narrow.astype(jnp.float32)


def reference(cotangent, out_weight, values, gate_input, conv_out, filter_taps):
    grad_mixed = jnp.dot(cotangent, out_weight.T, preferred_element_type=jnp.float32)
    gate_wide = gate_input.astype(jnp.float32)
    conv_wide = conv_out.astype(jnp.float32)
    grad_gate = (grad_mixed * conv_wide).astype(jnp.bfloat16)
    grad_conv = (grad_mixed * gate_wide).astype(jnp.bfloat16)
    gated = (gate_wide * conv_wide).astype(jnp.bfloat16)
    grad_weight = jnp.dot(gated.T, cotangent, preferred_element_type=jnp.float32)

    block_rows = TOK_DEV
    length, channels = grad_conv.shape
    count = length // block_rows
    period = 2 * block_rows
    dft_cos, dft_sin, back_cos, back_sin = make_tables(block_rows)
    fwd_cos = dft_cos.astype(jnp.float32)
    fwd_sin = dft_sin.astype(jnp.float32)
    inv_cos = back_cos.astype(jnp.float32)
    inv_sin = back_sin.astype(jnp.float32)

    def spectra(whole):
        blocks = whole.astype(jnp.float32).reshape(count, block_rows, channels)
        real_part = jnp.einsum("fb,nbc->nfc", fwd_cos[:, :block_rows], blocks, precision=lax.Precision.HIGHEST)
        imag_part = jnp.einsum("fb,nbc->nfc", fwd_sin[:, :block_rows], blocks, precision=lax.Precision.HIGHEST)
        return real_part, imag_part

    conv_re, conv_im = spectra(grad_conv)
    val_re, val_im = spectra(values)
    zero_blocks = jnp.zeros((count, period, channels), jnp.float32)
    conv_re_pad = jnp.concatenate([conv_re, zero_blocks], axis=0)
    conv_im_pad = jnp.concatenate([conv_im, zero_blocks], axis=0)
    padded_taps = jnp.concatenate([jnp.zeros((channels, block_rows), jnp.float32), filter_taps.astype(jnp.float32)], axis=1)

    def one_offset(carry, offset):
        sum_re, sum_im, lag_buf = carry
        window = lax.dynamic_slice_in_dim(padded_taps, offset * block_rows, period, 1)
        taps_re = high_dot(fwd_cos, window.T)
        taps_im = high_dot(fwd_sin, window.T)
        later_re = lax.dynamic_slice_in_dim(conv_re_pad, offset, count, 0)
        later_im = lax.dynamic_slice_in_dim(conv_im_pad, offset, count, 0)
        mix_re = round_wide(later_re * taps_re + later_im * taps_im)
        mix_im = round_wide(later_re * taps_im - later_im * taps_re)
        sum_re = sum_re + mix_re
        sum_im = sum_im + mix_im
        fil_re = jnp.sum(round_wide(val_re * later_re + val_im * later_im), axis=0)
        fil_im = jnp.sum(round_wide(val_re * later_im - val_im * later_re), axis=0)
        lag_part = high_dot(inv_cos, fil_re) + high_dot(inv_sin, fil_im)
        start = offset * block_rows
        current = lax.dynamic_slice_in_dim(lag_buf, start, period, 0)
        lag_buf = lax.dynamic_update_slice_in_dim(lag_buf, current + lag_part, start, 0)
        return (sum_re, sum_im, lag_buf), None

    init = (jnp.zeros((count, period, channels), jnp.float32), jnp.zeros((count, period, channels), jnp.float32), jnp.zeros(((count + 1) * block_rows, channels), jnp.float32))
    (sum_re, sum_im, lag_buf), _ = lax.scan(one_offset, init, jnp.arange(count, dtype=jnp.int32))
    value_blocks = jnp.einsum("af,nfc->nac", inv_cos[:block_rows], sum_re, precision=lax.Precision.HIGHEST) - jnp.einsum("af,nfc->nac", inv_sin[:block_rows], sum_im, precision=lax.Precision.HIGHEST)
    grad_value = value_blocks.reshape(length, channels).astype(jnp.bfloat16)
    grad_filter = lag_buf[block_rows:]
    return (grad_value, grad_gate, grad_filter.astype(jnp.float32), grad_weight)
```

```python
import functools

import jax
import jax.numpy as jnp
import numpy as np
from jax import lax
from jax.experimental import pallas as pl
from jax.experimental.pallas import tpu as pltpu
from jax.sharding import PartitionSpec as P

F32 = jnp.float32
BF16 = jnp.bfloat16


def make_tables(block_rows):
    n, period = block_rows, 2 * block_rows
    freq = np.arange(n)
    pos = np.arange(period)
    angle = 2.0 * np.pi * ((freq[:, None] * pos[None, :]) % period) / period
    cos = np.cos(angle)
    sin = np.sin(angle)
    sign = (1.0 - 2.0 * (freq % 2))[:, None]
    alt = (1.0 - 2.0 * (pos % 2))[None, :]
    narrow = lambda a: np.asarray(a, np.float32).astype(jnp.bfloat16)
    fwd_im = np.where(freq[:, None] == 0, alt, -sin)
    forward = np.concatenate([narrow(cos), narrow(fwd_im)], axis=0).T
    both = np.where(freq[:, None] == 0, 1.0, 2.0)
    back_cos = narrow(sign * cos / period).astype(np.float32) * both
    back_sin = narrow(-sign * sin / period).astype(np.float32) * both
    last = narrow(alt / period).astype(np.float32)
    first = freq[:, None] == 0
    value_back = np.concatenate([back_cos, np.where(first, last, -back_sin)], axis=0)[:, :n]
    filter_back = np.concatenate([back_cos, np.where(first, last, back_sin)], axis=0)
    return (
        np.ascontiguousarray(forward),
        np.ascontiguousarray(narrow(value_back)),
        np.ascontiguousarray(narrow(filter_back)),
    )


def dot(left, right, dims):
    return lax.dot_general(left, right, (dims, ((), ())), preferred_element_type=F32)


def call(body, out_shape, scratch, cost, *args):
    return pl.pallas_call(
        body,
        out_shape=out_shape,
        scratch_shapes=scratch,
        cost_estimate=pl.CostEstimate(flops=cost, bytes_accessed=1000000, transcendentals=0),
        compiler_params=pltpu.CompilerParams(vmem_limit_bytes=32 * 1024 * 1024),
    )(*args)


def pack_body(groups, per, w_ref, v_ref, out_ref, wide):
    rows, channels = w_ref.shape
    half = rows // 2
    lanes = v_ref.shape[1]
    w = w_ref[...].astype(F32)
    side = jnp.concatenate([w[:half, lanes:], w[half:, lanes:]], axis=1).astype(BF16)
    main = w_ref[:, :lanes]
    wide[channels:, :] = jnp.zeros((wide.shape[0] - channels, lanes), F32)
    wide[:channels, :] = v_ref[...].astype(F32)
    for g in range(groups):
        out_ref[g, :rows, :] = main
        out_ref[g, rows : rows + half, :] = side
        out_ref[g, rows + half :, :] = wide[per * g : per * g + 8, :].astype(BF16)


def terms_body(groups, f_ref, g_ref, o_ref, out_ref):
    lanes = g_ref.shape[1]
    rows = f_ref.shape[0] // groups
    half = rows // 2
    gated = (g_ref[...].astype(F32) * o_ref[...].astype(F32)).astype(BF16)
    f = f_ref[...]
    main = dot(f, gated[:lanes], ((1,), (1,)))
    out_ref[:, :rows, :] = main.astype(BF16).reshape(groups, rows, lanes)
    rest = gated[lanes:]
    zero = jnp.zeros_like(rest)
    f3 = f.reshape(groups, rows, lanes)
    low = f3[:, :half].reshape(groups * half, lanes)
    high = f3[:, half:].reshape(groups * half, lanes)
    side = dot(low, jnp.concatenate([rest, zero], axis=0), ((1,), (1,)))
    side = side + dot(high, jnp.concatenate([zero, rest], axis=0), ((1,), (1,)))
    out_ref[:, rows:, :] = side.astype(BF16).reshape(groups, half, lanes)


def front_body(groups, per, w_ref, f_ref, g_ref, o_ref, gate_ref, out_ref, wide):
    lanes = g_ref.shape[1]
    channels = g_ref.shape[0]
    rows = f_ref.shape[0] // groups
    half = rows // 2
    f = f_ref[...]
    main = dot(w_ref[:, :rows, :].reshape(groups * rows, lanes), f, ((0,), (0,)))
    side_w = w_ref[:, rows : rows + half, :].reshape(groups * half, lanes)
    f3 = f.reshape(groups, rows, lanes)
    low = dot(side_w, f3[:, :half].reshape(groups * half, lanes), ((0,), (0,)))
    high = dot(side_w, f3[:, half:].reshape(groups * half, lanes), ((0,), (0,)))
    mixed = jnp.concatenate([main, low[: lanes // 2] + high[lanes // 2 :]], axis=0)
    gate_ref[...] = (mixed * o_ref[...].astype(F32)).astype(BF16)
    wide[channels:, :] = jnp.zeros((wide.shape[0] - channels, lanes), F32)
    wide[:channels, :] = mixed * g_ref[...].astype(F32)
    for g in range(groups):
        out_ref[g] = wide[per * g : per * g + 8, :].astype(BF16)


def spectra_body(wv_ref, taps_ref, table_ref, t_ref, v_ref):
    groups = wv_ref.shape[0]
    lanes = wv_ref.shape[2]
    rows = groups * 8
    table = table_ref[...]
    first = lax.broadcasted_iota(jnp.int32, (rows, lanes), 1) == 0
    val = dot(wv_ref[:, wv_ref.shape[1] - 8 :, :].reshape(rows, lanes), table[:lanes], ((1,), (0,)))
    val_re, val_im = val[:, :lanes], val[:, lanes:]
    v_ref[0] = val_re
    v_ref[1] = jnp.where(first, 0.0, val_im)
    v_ref[2] = jnp.where(first, val_im, val_re)
    taps = taps_ref[...].reshape(rows, lanes)
    upper = dot(taps, table[lanes:], ((1,), (0,)))
    lower = dot(taps, table[:lanes], ((1,), (0,)))
    lower = jnp.concatenate([jnp.zeros((8, 2 * lanes), F32), lower[: rows - 8]], axis=0)
    spec = upper + lower
    taps_re, taps_im = spec[:, :lanes], spec[:, lanes:]
    t_ref[0] = taps_re
    t_ref[1] = jnp.where(first, 0.0, taps_im)
    t_ref[2] = jnp.where(first, taps_im, -taps_re)


def mix_body(count, g_ref, t_ref, v_ref, table_ref, vback_ref, fback_ref, out_ref, conv, vmix, fmix):
    lanes = g_ref.shape[2]
    rows = count * 8
    conv[...] = dot(g_ref[...].reshape(rows, lanes), table_ref[...], ((1,), (0,)))
    tile = 8
    for base in range(0, count, tile):
        zero = jnp.zeros((8, lanes), F32)
        acc = [[zero] * 4 for _ in range(tile)]
        for shift in range(count - base):
            at = pl.ds(8 * shift, 8)
            tr, tb, td = t_ref[0, at], t_ref[1, at], t_ref[2, at]
            vr, vb, vd = v_ref[0, at], v_ref[1, at], v_ref[2, at]
            for r in range(min(tile, count - base - shift)):
                place = pl.ds(8 * (base + r + shift), 8)
                cr = conv[place, :lanes]
                ci = conv[place, lanes:]
                a = acc[r]
                acc[r] = [
                    a[0] + cr * tr + ci * tb,
                    a[1] + cr * tb + ci * td,
                    a[2] + cr * vr + ci * vb,
                    a[3] + ci * vd - cr * vb,
                ]
        for r in range(tile):
            place = pl.ds(8 * (base + r), 8)
            vmix[place, :lanes] = acc[r][0]
            vmix[place, lanes:] = acc[r][1]
            fmix[place, :lanes] = acc[r][2]
            fmix[place, lanes:] = acc[r][3]
    fmix[rows:, :] = jnp.zeros((8, 2 * lanes), F32)
    value = dot(vmix[...].astype(BF16), vback_ref[...], ((1,), (0,)))
    fback = fback_ref[...]
    late = dot(fmix[:rows].astype(BF16), fback[:, lanes:], ((1,), (0,)))
    early = dot(fmix[8:].astype(BF16), fback[:, :lanes], ((1,), (0,)))
    out_ref[:, :8, :] = value.astype(BF16).reshape(count, 8, lanes)
    out_ref[:, 8:, :] = (late + early).astype(BF16).reshape(count, 8, lanes)


def sum_body(in_ref, out_ref):
    groups, packed, lanes = in_ref.shape
    rows = out_ref.shape[0]
    half = rows // 2
    total = in_ref[0].astype(F32)
    for g in range(1, groups):
        total = total + in_ref[g].astype(F32)
    out_ref[:, :lanes] = total[:rows]
    side = total[rows:]
    rest = out_ref.shape[1] - lanes
    out_ref[:half, lanes:] = side[:, :rest]
    out_ref[half:, lanes:] = side[:, rest:]


def finish_body(per, in_ref, value_ref, filter_ref, wide):
    groups = in_ref.shape[0]
    channels = value_ref.shape[0]
    for g in range(groups):
        wide[per * g : per * g + 8, :] = in_ref[g, :8, :].astype(F32)
    value_ref[...] = wide[:channels, :].astype(BF16)
    for g in range(groups):
        wide[per * g : per * g + 8, :] = in_ref[g, 8:, :].astype(F32)
    filter_ref[...] = wide[:channels, :]


def body(cotangent, out_weight, values, gate_input, conv_out, filter_taps):
    block_rows, channels = values.shape
    count = lax.axis_size("seq")
    parts = lax.axis_size("fsdp")
    rows = out_weight.shape[1]
    features = rows * count
    per = channels // count
    forward, value_back, filter_back = (jnp.asarray(t) for t in make_tables(block_rows))
    cot, weight, vals = cotangent.T, out_weight.T, values.T
    gate, conv = gate_input.T, conv_out.T
    shape = jax.ShapeDtypeStruct
    exchange = lambda x, axis: lax.all_to_all(x, axis, 0, 0)
    packed = rows + rows // 2
    wide = [pltpu.VMEM((channels + 8, block_rows), F32)]

    cots = exchange(jnp.broadcast_to(cot[None], (parts, *cot.shape)), "fsdp")
    full = cots.reshape(features, block_rows)
    sent = call(
        functools.partial(pack_body, count, per),
        shape((count, packed + 8, block_rows), BF16), wide, 1000, weight, vals,
    )
    got = exchange(sent, "seq")
    terms = call(
        functools.partial(terms_body, count),
        shape((count, packed, block_rows), BF16), [], 2 * features * channels * block_rows, full, gate, conv,
    )
    terms = exchange(terms, "seq")
    grad_gate, mine = call(
        functools.partial(front_body, count, per),
        (shape((channels, block_rows), BF16), shape((count, 8, block_rows), BF16)),
        wide, 2 * features * channels * block_rows, got, full, gate, conv,
    )
    mine = exchange(mine, "seq")
    own = lax.dynamic_slice_in_dim(filter_taps, lax.axis_index("seq") * per, per, 0)
    own = jnp.transpose(own.reshape(per, count, block_rows), (1, 0, 2))
    own = jnp.pad(own, ((0, 0), (0, 8 - per), (0, 0)))
    form = shape((3, count * 8, block_rows), F32)
    tap_forms, val_forms = call(
        spectra_body, (form, form), [], 6 * count * 8 * block_rows * 2 * block_rows, got, own, forward
    )
    both = call(
        functools.partial(mix_body, count),
        shape((count, 16, block_rows), BF16),
        [
            pltpu.VMEM((count * 8, 2 * block_rows), F32),
            pltpu.VMEM((count * 8, 2 * block_rows), F32),
            pltpu.VMEM((count * 8 + 8, 2 * block_rows), F32),
        ],
        8 * count * 8 * block_rows * 2 * block_rows,
        mine, tap_forms, val_forms, forward[:block_rows], value_back, filter_back,
    )
    both = exchange(both, "seq")
    grad_weight = call(sum_body, shape((rows, channels), F32), [], count * packed * block_rows, terms)
    grad_value, grad_filter = call(
        functools.partial(finish_body, per),
        (shape((channels, block_rows), BF16), shape((channels, block_rows), F32)),
        wide, 1000, both,
    )
    return (grad_value.T, grad_gate.T, grad_filter.T, grad_weight.T)


def solution(mesh):
    in_specs = (
        P("seq", "fsdp"),
        P("fsdp", "seq"),
        P("seq", "fsdp"),
        P("seq", "fsdp"),
        P("seq", "fsdp"),
        P("fsdp", None),
    )
    out_specs = (P("seq", "fsdp"), P("seq", "fsdp"), P("seq", "fsdp"), P("fsdp", "seq"))
    return jax.shard_map(body, mesh=mesh, in_specs=in_specs, out_specs=out_specs, check_vma=False)
```

```python
import functools

import jax
import jax.numpy as jnp
import numpy as np
from jax import lax
from jax.experimental import pallas as pl
from jax.experimental.pallas import tpu as pltpu
from jax.sharding import PartitionSpec as P

F32 = jnp.float32
BF16 = jnp.bfloat16


def make_tables(block_rows):
    n, period = block_rows, 2 * block_rows
    freq = np.arange(n)
    pos = np.arange(period)
    angle = 2.0 * np.pi * ((freq[:, None] * pos[None, :]) % period) / period
    cos = np.cos(angle)
    sin = np.sin(angle)
    sign = (1.0 - 2.0 * (freq % 2))[:, None]
    alt = (1.0 - 2.0 * (pos % 2))[None, :]
    narrow = lambda a: np.asarray(a, np.float32).astype(jnp.bfloat16)
    fwd_im = np.where(freq[:, None] == 0, alt, -sin)
    forward = np.concatenate([narrow(cos), narrow(fwd_im)], axis=0).T
    both = np.where(freq[:, None] == 0, 1.0, 2.0)
    back_cos = narrow(sign * cos / period).astype(np.float32) * both
    back_sin = narrow(-sign * sin / period).astype(np.float32) * both
    last = narrow(alt / period).astype(np.float32)
    first = freq[:, None] == 0
    value_back = np.concatenate([back_cos, np.where(first, last, -back_sin)], axis=0)[:, :n]
    filter_back = np.concatenate([back_cos, np.where(first, last, back_sin)], axis=0)
    return (
        np.ascontiguousarray(forward),
        np.ascontiguousarray(narrow(value_back)),
        np.ascontiguousarray(narrow(filter_back)),
    )


def dot(left, right, dims):
    return lax.dot_general(left, right, (dims, ((), ())), preferred_element_type=F32)


def call(body, out_shape, scratch, cost, *args):
    return pl.pallas_call(
        body,
        out_shape=out_shape,
        scratch_shapes=scratch,
        cost_estimate=pl.CostEstimate(flops=cost, bytes_accessed=1000000, transcendentals=0),
        compiler_params=pltpu.CompilerParams(vmem_limit_bytes=32 * 1024 * 1024),
    )(*args)


def pack_body(groups, per, w_ref, v_ref, out_ref, wide):
    rows, channels = w_ref.shape
    half = rows // 2
    low = 2 * half // 3
    lanes = v_ref.shape[1]
    w = w_ref[...].astype(F32)
    wide[channels:, :] = jnp.zeros((wide.shape[0] - channels, lanes), F32)
    wide[:channels, :] = v_ref[...].astype(F32)
    parts = []
    for h in range(2):
        mine = w[h * half : (h + 1) * half]
        high = jnp.concatenate([mine[low:, lanes:], jnp.zeros((2 * low - half, channels - lanes), F32)], axis=0)
        side = jnp.concatenate([mine[:low, lanes:], high], axis=1)
        parts.append(jnp.concatenate([mine[:, :lanes], side], axis=0).astype(BF16))
    for g in range(groups):
        out_ref[g, : half + low, :] = parts[g % 2]
        out_ref[g, half + low :, :] = wide[per * g : per * g + 8, :].astype(BF16)


def terms_body(groups, masks, near_ref, far_ref, g_ref, o_ref, full_ref, keep_ref, send_ref):
    lanes = g_ref.shape[1]
    channels = g_ref.shape[0]
    here = lax.axis_index("fsdp")
    core = lax.rem(lax.axis_index("seq"), 2)
    for slot, mask in enumerate(masks):
        at = pl.multiple_of(jnp.bitwise_xor(here, mask) * channels, channels)
        source = near_ref if slot < len(masks) // 2 else far_ref
        full_ref[pl.ds(at, channels), :] = source[slot % (len(masks) // 2)]
    rows = full_ref.shape[0] // groups
    half = rows // 2
    gated = (g_ref[...].astype(F32) * o_ref[...].astype(F32)).astype(BF16)
    f = full_ref[...]
    main = dot(f, gated[:lanes], ((1,), (1,))).astype(BF16).reshape(groups, rows, lanes)
    rest = gated[lanes:]
    zero = jnp.zeros_like(rest)
    f3 = f.reshape(groups, rows, lanes)
    low = f3[:, :half].reshape(groups * half, lanes)
    high = f3[:, half:].reshape(groups * half, lanes)
    side = dot(low, jnp.concatenate([rest, zero], axis=0), ((1,), (1,)))
    side = side + dot(high, jnp.concatenate([zero, rest], axis=0), ((1,), (1,)))
    side = side.astype(BF16).reshape(groups, half, lanes)
    cut = keep_ref.shape[1]

    def put(first_ref, second_ref):
        first_ref[...] = main[:, :cut]
        second_ref[:, : rows - cut, :] = main[:, cut:]
        second_ref[:, rows - cut : rows - cut + half, :] = side
        second_ref[:, rows - cut + half :, :] = jnp.zeros((groups, 2 * cut - rows - half, lanes), BF16)

    @pl.when(core == 0)
    def _():
        put(keep_ref, send_ref)

    @pl.when(core == 1)
    def _():
        put(send_ref, keep_ref)


def front_body(groups, per, own_ref, other_ref, f_ref, g_ref, o_ref, gate_ref, out_ref, weight, wide):
    lanes = g_ref.shape[1]
    channels = g_ref.shape[0]
    rows = f_ref.shape[0] // groups
    half = rows // 2
    low = 2 * half // 3
    core = lax.rem(lax.axis_index("seq"), 2)
    for source, which in ((own_ref, core), (other_ref, 1 - core)):
        for g in range(groups):
            at = pl.multiple_of(rows * g + half * which, 8)
            weight[pl.ds(at, half), :lanes] = source[g, :half, :]
            side = source[g, half : half + low, :]
            weight[pl.ds(at, low), lanes:] = side
            turned = jnp.concatenate([side[: half - low, lanes // 2 :], side[: half - low, : lanes // 2]], axis=1)
            weight[pl.ds(at + low, half - low), lanes:] = turned
    mixed = dot(weight[...], f_ref[...], ((0,), (0,)))[:channels]
    gate_ref[...] = (mixed * o_ref[...].astype(F32)).astype(BF16)
    wide[channels:, :] = jnp.zeros((wide.shape[0] - channels, lanes), F32)
    wide[:channels, :] = mixed * g_ref[...].astype(F32)
    for g in range(groups):
        out_ref[g] = wide[per * g : per * g + 8, :].astype(BF16)


def spectra_body(wv_ref, taps_ref, table_ref, t_ref, v_ref):
    groups = wv_ref.shape[0]
    lanes = wv_ref.shape[2]
    rows = groups * 8
    table = table_ref[...]
    first = lax.broadcasted_iota(jnp.int32, (rows, lanes), 1) == 0
    val = dot(wv_ref[:, wv_ref.shape[1] - 8 :, :].reshape(rows, lanes), table[:lanes], ((1,), (0,)))
    val_re, val_im = val[:, :lanes], val[:, lanes:]
    v_ref[0] = val_re
    v_ref[1] = jnp.where(first, 0.0, val_im)
    v_ref[2] = jnp.where(first, val_im, val_re)
    taps = taps_ref[...].reshape(rows, lanes)
    upper = dot(taps, table[lanes:], ((1,), (0,)))
    lower = dot(taps, table[:lanes], ((1,), (0,)))
    lower = jnp.concatenate([jnp.zeros((8, 2 * lanes), F32), lower[: rows - 8]], axis=0)
    spec = upper + lower
    taps_re, taps_im = spec[:, :lanes], spec[:, lanes:]
    t_ref[0] = taps_re
    t_ref[1] = jnp.where(first, 0.0, taps_im)
    t_ref[2] = jnp.where(first, taps_im, -taps_re)


def mix_body(
    count, g_ref, t_ref, v_ref, table_ref, vback_ref, fback_ref, keep_ref, came_ref, out_ref, conv, vmix, fmix
):
    lanes = g_ref.shape[2]
    out_ref[:, 16:, :] = (keep_ref[...].astype(F32) + came_ref[...].astype(F32)).astype(BF16)
    rows = count * 8
    conv[...] = dot(g_ref[...].reshape(rows, lanes), table_ref[...], ((1,), (0,)))
    tile = 8
    for base in range(0, count, tile):
        zero = jnp.zeros((8, lanes), F32)
        acc = [[zero] * 4 for _ in range(tile)]
        for shift in range(count - base):
            at = pl.ds(8 * shift, 8)
            tr, tb, td = t_ref[0, at], t_ref[1, at], t_ref[2, at]
            vr, vb, vd = v_ref[0, at], v_ref[1, at], v_ref[2, at]
            for r in range(min(tile, count - base - shift)):
                place = pl.ds(8 * (base + r + shift), 8)
                cr = conv[place, :lanes]
                ci = conv[place, lanes:]
                a = acc[r]
                acc[r] = [
                    a[0] + cr * tr + ci * tb,
                    a[1] + cr * tb + ci * td,
                    a[2] + cr * vr + ci * vb,
                    a[3] + ci * vd - cr * vb,
                ]
        for r in range(tile):
            place = pl.ds(8 * (base + r), 8)
            vmix[place, :lanes] = acc[r][0]
            vmix[place, lanes:] = acc[r][1]
            fmix[place, :lanes] = acc[r][2]
            fmix[place, lanes:] = acc[r][3]
    fmix[rows:, :] = jnp.zeros((8, 2 * lanes), F32)
    value = dot(vmix[...].astype(BF16), vback_ref[...], ((1,), (0,)))
    fback = fback_ref[...]
    late = dot(fmix[:rows].astype(BF16), fback[:, lanes:], ((1,), (0,)))
    early = dot(fmix[8:].astype(BF16), fback[:, :lanes], ((1,), (0,)))
    out_ref[:, :8, :] = value.astype(BF16).reshape(count, 8, lanes)
    out_ref[:, 8:16, :] = (late + early).astype(BF16).reshape(count, 8, lanes)


def finish_body(per, in_ref, value_ref, filter_ref, weight_ref, wide):
    groups, packed, lanes = in_ref.shape
    channels = value_ref.shape[0]
    for g in range(groups):
        wide[per * g : per * g + 8, :] = in_ref[g, :8, :].astype(F32)
    value_ref[...] = wide[:channels, :].astype(BF16)
    for g in range(groups):
        wide[per * g : per * g + 8, :] = in_ref[g, 8:16, :].astype(F32)
    filter_ref[...] = wide[:channels, :]
    rows = weight_ref.shape[0]
    half = rows // 2
    cut = packed - 16
    first, second = in_ref[0, 16:, :].astype(F32), in_ref[1, 16:, :].astype(F32)
    for g in range(2, groups, 2):
        first = first + in_ref[g, 16:, :].astype(F32)
        second = second + in_ref[g + 1, 16:, :].astype(F32)
    weight_ref[:cut, :lanes] = first
    weight_ref[cut:, :lanes] = second[: rows - cut]
    side = second[rows - cut : rows - cut + half]
    rest = channels - lanes
    weight_ref[:half, lanes:] = side[:, :rest]
    weight_ref[half:, lanes:] = side[:, rest:]


def body(cotangent, out_weight, values, gate_input, conv_out, filter_taps):
    block_rows, channels = values.shape
    count = lax.axis_size("seq")
    parts = lax.axis_size("fsdp")
    rows = out_weight.shape[1]
    features = rows * count
    per = channels // count
    forward, value_back, filter_back = (jnp.asarray(t) for t in make_tables(block_rows))
    cot, weight, vals = cotangent.T, out_weight.T, values.T
    gate, conv = gate_input.T, conv_out.T
    shape = jax.ShapeDtypeStruct
    exchange = lambda x, axis: lax.all_to_all(x, axis, 0, 0)
    half = rows // 2
    cut = (3 * half + 15) // 16 * 8
    wide = [pltpu.VMEM((channels + 8, block_rows), F32)]
    swap = lambda x: lax.ppermute(x, "seq", [(i, i ^ 1) for i in range(count)])
    cross = lambda x, mask: lax.ppermute(x, "fsdp", [(i, i ^ mask) for i in range(parts)])

    sent = call(
        functools.partial(pack_body, count, per),
        shape((count, half + 2 * half // 3 + 8, block_rows), BF16), wide, 1000, weight, vals,
    )
    got = exchange(sent, "seq")
    pair = jnp.stack([cot, cross(cot, 1)])
    near = jnp.concatenate([pair, cross(pair, 3)])
    far = cross(near, 4)
    half_terms = shape((count, cut, block_rows), BF16)
    full, keep, give = call(
        functools.partial(terms_body, count, (0, 1, 3, 2, 4, 5, 7, 6)),
        (shape((features, block_rows), BF16), half_terms, half_terms),
        [], 2 * features * channels * block_rows, near, far, gate, conv,
    )
    came = swap(give)
    other = swap(got)
    grad_gate, mine = call(
        functools.partial(front_body, count, per),
        (shape((channels, block_rows), BF16), shape((count, 8, block_rows), BF16)),
        [pltpu.VMEM((features, 2 * block_rows), BF16), *wide],
        2 * features * channels * block_rows, got, other, full, gate, conv,
    )
    mine = exchange(mine, "seq")
    own = lax.dynamic_slice_in_dim(filter_taps, lax.axis_index("seq") * per, per, 0)
    own = jnp.transpose(own.reshape(per, count, block_rows), (1, 0, 2))
    own = jnp.pad(own, ((0, 0), (0, 8 - per), (0, 0)))
    form = shape((3, count * 8, block_rows), F32)
    tap_forms, val_forms = call(
        spectra_body, (form, form), [], 6 * count * 8 * block_rows * 2 * block_rows, got, own, forward
    )
    both = call(
        functools.partial(mix_body, count),
        shape((count, 16 + cut, block_rows), BF16),
        [
            pltpu.VMEM((count * 8, 2 * block_rows), F32),
            pltpu.VMEM((count * 8, 2 * block_rows), F32),
            pltpu.VMEM((count * 8 + 8, 2 * block_rows), F32),
        ],
        8 * count * 8 * block_rows * 2 * block_rows,
        mine, tap_forms, val_forms, forward[:block_rows], value_back, filter_back, keep, came,
    )
    both = exchange(both, "seq")
    grad_value, grad_filter, grad_weight = call(
        functools.partial(finish_body, per),
        (shape((channels, block_rows), BF16), shape((channels, block_rows), F32), shape((rows, channels), F32)),
        wide, 1000, both,
    )
    return (grad_value.T, grad_gate.T, grad_filter.T, grad_weight.T)


def solution(mesh):
    in_specs = (
        P("seq", "fsdp"),
        P("fsdp", "seq"),
        P("seq", "fsdp"),
        P("seq", "fsdp"),
        P("seq", "fsdp"),
        P("fsdp", None),
    )
    out_specs = (P("seq", "fsdp"), P("seq", "fsdp"), P("seq", "fsdp"), P("fsdp", "seq"))
    return jax.shard_map(body, mesh=mesh, in_specs=in_specs, out_specs=out_specs, check_vma=False)
```

```python
import functools

import jax
import jax.numpy as jnp
import numpy as np
from jax import lax
from jax.experimental import pallas as pl
from jax.experimental.pallas import tpu as pltpu
from jax.sharding import PartitionSpec as P

F32 = jnp.float32
BF16 = jnp.bfloat16


def make_tables(block_rows):
    n, period = block_rows, 2 * block_rows
    freq = np.arange(n)
    pos = np.arange(period)
    angle = 2.0 * np.pi * ((freq[:, None] * pos[None, :]) % period) / period
    cos = np.cos(angle)
    sin = np.sin(angle)
    sign = (1.0 - 2.0 * (freq % 2))[:, None]
    alt = (1.0 - 2.0 * (pos % 2))[None, :]
    narrow = lambda a: np.asarray(a, np.float32).astype(jnp.bfloat16)
    fwd_im = np.where(freq[:, None] == 0, alt, -sin)
    forward = np.concatenate([narrow(cos), narrow(fwd_im)], axis=0).T
    both = np.where(freq[:, None] == 0, 1.0, 2.0)
    back_cos = narrow(sign * cos / period).astype(np.float32) * both
    back_sin = narrow(-sign * sin / period).astype(np.float32) * both
    last = narrow(alt / period).astype(np.float32)
    first = freq[:, None] == 0
    value_back = np.concatenate([back_cos, np.where(first, last, -back_sin)], axis=0)[:, :n]
    filter_back = np.concatenate([back_cos, np.where(first, last, back_sin)], axis=0)
    return (
        np.ascontiguousarray(forward),
        np.ascontiguousarray(narrow(value_back)),
        np.ascontiguousarray(narrow(filter_back)),
    )


def dot(left, right, dims):
    return lax.dot_general(left, right, (dims, ((), ())), preferred_element_type=F32)


def call(body, out_shape, scratch, cost, *args, room=32 * 1024 * 1024, **specs):
    return pl.pallas_call(
        body,
        out_shape=out_shape,
        scratch_shapes=scratch,
        **specs,
        cost_estimate=pl.CostEstimate(flops=cost, bytes_accessed=1000000, transcendentals=0),
        compiler_params=pltpu.CompilerParams(vmem_limit_bytes=room),
    )(*args)


def pack_body(chips, per, w_ref, v_ref, out_ref, wide):
    rows, channels = w_ref.shape
    half = rows // 2
    lanes = v_ref.shape[1]
    main = w_ref[:, :lanes]
    w = w_ref[...].astype(F32)
    side = jnp.concatenate([w[:half, lanes:], w[half:, lanes:]], axis=1).astype(BF16)
    wide[channels:, :] = jnp.zeros((wide.shape[0] - channels, lanes), F32)
    wide[:channels, :] = v_ref[...].astype(F32)
    for chip in range(chips):
        out_ref[chip, :rows, :] = main
        out_ref[chip, rows : rows + half, :] = side
        for core in range(2):
            at = rows + half + 8 * core
            begin = per * (2 * chip + core)
            out_ref[chip, at : at + 8, :] = wide[begin : begin + 8, :].astype(BF16)


def terms_body(groups, masks, near_ref, far_ref, g_ref, o_ref, keep_ref, send_ref):
    lanes = g_ref.shape[1]
    channels = g_ref.shape[0]
    here = lax.axis_index("fsdp")
    core = lax.rem(lax.axis_index("seq"), 2)
    share = groups // len(masks)
    rows = channels // share
    half = rows // 2
    gated = (g_ref[...].astype(F32) * o_ref[...].astype(F32)).astype(BF16)
    rest = gated[lanes:]
    zero = jnp.zeros_like(rest)
    lower = jnp.concatenate([rest, zero], axis=0)
    upper = jnp.concatenate([zero, rest], axis=0)
    blocks = len(masks) // 2
    for part, source in enumerate((near_ref, far_ref)):
        f = source[...].reshape(blocks * channels, lanes)
        main = dot(f, gated[:lanes], ((1,), (1,))).astype(BF16).reshape(blocks * share, rows, lanes)
        f3 = f.reshape(blocks * share, rows, lanes)
        low = f3[:, :half].reshape(blocks * share * half, lanes)
        high = f3[:, half:].reshape(blocks * share * half, lanes)
        side = dot(low, lower, ((1,), (1,))) + dot(high, upper, ((1,), (1,)))
        side = side.astype(BF16).reshape(blocks * share, half, lanes)

        def put(*refs):
            for i in range(blocks):
                first = jnp.bitwise_xor(here, masks[part * blocks + i]) * (share // 2)
                for q in range(share):
                    refs[q % 2][first + q // 2, :rows, :] = main[i * share + q]
                    refs[q % 2][first + q // 2, rows:, :] = side[i * share + q]

        @pl.when(core == 0)
        def _():
            put(keep_ref, send_ref)

        @pl.when(core == 1)
        def _():
            put(send_ref, keep_ref)


def front_body(groups, per, masks, own_ref, other_ref, near_ref, far_ref, g_ref, o_ref, gate_ref, out_ref, weight, wide):
    lanes = g_ref.shape[1]
    channels = g_ref.shape[0]
    here = lax.axis_index("fsdp")
    core = lax.rem(lax.axis_index("seq"), 2)
    share = groups // len(masks)
    rows = channels // share
    half = rows // 2
    for source, which in ((own_ref, core), (other_ref, 1 - core)):
        for slot in range(len(masks)):
            for q in range(share // 2):
                chip = jnp.bitwise_xor(here, masks[slot]) * (share // 2) + q
                at = pl.multiple_of(rows * (slot * share + 2 * q + which), 8)
                weight[pl.ds(at, rows), :lanes] = source[chip, :rows, :]
                side = source[chip, rows : rows + half, :]
                weight[pl.ds(at, half), lanes:] = side
                turned = jnp.concatenate([side[:, lanes // 2 :], side[:, : lanes // 2]], axis=1)
                weight[pl.ds(at + half, half), lanes:] = turned
    size = groups * rows // 2
    mixed = dot(weight[:size], near_ref[...].reshape(size, lanes), ((0,), (0,)))
    mixed = (mixed + dot(weight[size:], far_ref[...].reshape(size, lanes), ((0,), (0,))))[:channels]
    gate_ref[...] = (mixed * o_ref[...].astype(F32)).astype(BF16)
    wide[channels:, :] = jnp.zeros((wide.shape[0] - channels, lanes), F32)
    wide[:channels, :] = mixed * g_ref[...].astype(F32)
    for chip in range(groups // 2):
        for c in range(2):
            begin = per * (2 * chip + c)
            out_ref[chip, 8 * c : 8 * c + 8, :] = wide[begin : begin + 8, :].astype(BF16)


def in_order(own_ref, other_ref, row, blocks):
    core = lax.rem(lax.axis_index("seq"), 2)
    at = pl.multiple_of(row + 8 * core, 8)
    for chip in range(own_ref.shape[0]):
        blocks[pl.ds(pl.multiple_of(16 * chip + 8 * core, 8), 8), :] = own_ref[chip, pl.ds(at, 8), :]
        blocks[pl.ds(pl.multiple_of(16 * chip + 8 * (1 - core), 8), 8), :] = other_ref[chip, pl.ds(at, 8), :]


def join_body(keep_ref, came_ref, out_ref):
    out_ref[...] = (keep_ref[...].astype(F32) + came_ref[...].astype(F32)).astype(BF16)


def spectra_body(per, own_ref, other_ref, taps_ref, table_ref, vback_ref, fback_ref, out_ref, near, blocks, sem):
    groups = 2 * own_ref.shape[0]
    lanes = own_ref.shape[2]
    window = near.shape[0]
    start = lax.axis_index("seq") * per
    base = pl.multiple_of(jnp.minimum(start // 8 * 8, taps_ref.shape[0] - window), 8)
    copy = pltpu.make_async_copy(taps_ref.at[pl.ds(base, window)], near, sem)
    copy.start()
    rows = groups * 8
    table = table_ref[...]
    first = lax.broadcasted_iota(jnp.int32, (rows, lanes), 1) == 0
    in_order(own_ref, other_ref, own_ref.shape[1] - 16, blocks)
    val = dot(blocks[...], table[:lanes], ((1,), (0,)))
    val_re, val_im = val[:, :lanes], val[:, lanes:]
    out_ref[3] = val_re
    out_ref[4] = jnp.where(first, 0.0, val_im)
    out_ref[5] = jnp.where(first, val_im, val_re)
    copy.wait()
    own = pltpu.roll(near[...].astype(F32), window - (start - base), 0)[:8].astype(BF16)
    taps = jnp.concatenate([own[:, i * lanes : (i + 1) * lanes] for i in range(groups)], axis=0)
    upper = dot(taps, table[lanes:], ((1,), (0,)))
    lower = dot(taps, table[:lanes], ((1,), (0,)))
    lower = jnp.concatenate([jnp.zeros((8, 2 * lanes), F32), lower[: rows - 8]], axis=0)
    spec = upper + lower
    taps_re, taps_im = spec[:, :lanes], spec[:, lanes:]
    out_ref[0] = taps_re
    out_ref[1] = jnp.where(first, 0.0, taps_im)
    out_ref[2] = jnp.where(first, taps_im, -taps_re)
    out_ref[6] = jnp.concatenate([table[:lanes, :lanes], table[:lanes, lanes:]], axis=0).astype(F32)
    out_ref[7] = vback_ref[...].astype(F32)
    out_ref[8] = fback_ref[:, :lanes].astype(F32)
    out_ref[9] = fback_ref[:, lanes:].astype(F32)


def mix_body(count, own_ref, other_ref, forms_ref, keep_ref, send_ref, blocks, conv, vmix, fmix):
    lanes = own_ref.shape[2]
    rows = count * 8
    in_order(own_ref, other_ref, 0, blocks)
    g = blocks[...]
    conv[:, :lanes] = dot(g, forms_ref[6, :lanes].astype(BF16), ((1,), (0,)))
    conv[:, lanes:] = dot(g, forms_ref[6, lanes:].astype(BF16), ((1,), (0,)))
    tile = 8
    for base in range(0, count, tile):
        zero = jnp.zeros((8, lanes), F32)
        acc = [[zero] * 4 for _ in range(tile)]
        for shift in range(count - base):
            at = pl.ds(8 * shift, 8)
            tr, tb, td = forms_ref[0, at], forms_ref[1, at], forms_ref[2, at]
            vr, vb, vd = forms_ref[3, at], forms_ref[4, at], forms_ref[5, at]
            for r in range(min(tile, count - base - shift)):
                place = pl.ds(8 * (base + r + shift), 8)
                cr = conv[place, :lanes]
                ci = conv[place, lanes:]
                a = acc[r]
                acc[r] = [
                    a[0] + cr * tr + ci * tb,
                    a[1] + cr * tb + ci * td,
                    a[2] + cr * vr + ci * vb,
                    a[3] + ci * vd - cr * vb,
                ]
        for r in range(tile):
            place = pl.ds(8 * (base + r), 8)
            vmix[place, :lanes] = acc[r][0]
            vmix[place, lanes:] = acc[r][1]
            fmix[place, :lanes] = acc[r][2]
            fmix[place, lanes:] = acc[r][3]
    fmix[rows:, :] = jnp.zeros((8, 2 * lanes), F32)
    value = dot(vmix[...].astype(BF16), forms_ref[7].astype(BF16), ((1,), (0,)))
    late = dot(fmix[:rows].astype(BF16), forms_ref[9].astype(BF16), ((1,), (0,)))
    early = dot(fmix[8:].astype(BF16), forms_ref[8].astype(BF16), ((1,), (0,)))
    value = value.astype(BF16).reshape(count, 8, lanes)
    lags = (late + early).astype(BF16).reshape(count, 8, lanes)

    def put(*refs):
        for i in range(count):
            refs[i % 2][i // 2, :8, :] = value[i]
            refs[i % 2][i // 2, 8:, :] = lags[i]

    core = lax.rem(lax.axis_index("seq"), 2)

    @pl.when(core == 0)
    def _():
        put(keep_ref, send_ref)

    @pl.when(core == 1)
    def _():
        put(send_ref, keep_ref)


def last_body(keep_ref, came_ref, joined_ref, out_ref):
    core = lax.rem(lax.axis_index("seq"), 2)
    out_ref[:, pl.ds(pl.multiple_of(16 * core, 8), 16), :] = keep_ref[...]
    out_ref[:, pl.ds(pl.multiple_of(16 * (1 - core), 8), 16), :] = came_ref[...]
    out_ref[:, 32:, :] = joined_ref[...]


def finish_body(per, in_ref, value_ref, filter_ref, weight_ref, wide):
    chips, packed, lanes = in_ref.shape
    channels = value_ref.shape[0]
    for row, target in ((0, value_ref), (8, filter_ref)):
        for chip in range(chips):
            for c in range(2):
                at = per * (2 * chip + c)
                wide[at : at + 8, :] = in_ref[chip, row + 16 * c : row + 16 * c + 8, :].astype(F32)
        target[...] = wide[:channels, :].astype(target.dtype)
    rows = weight_ref.shape[0]
    half = rows // 2
    total = in_ref[0, 32:, :].astype(F32)
    for chip in range(1, chips):
        total = total + in_ref[chip, 32:, :].astype(F32)
    weight_ref[:, :lanes] = total[:rows]
    rest = channels - lanes
    weight_ref[:half, lanes:] = total[rows:, :rest]
    weight_ref[half:, lanes:] = total[rows:, rest:]


def body(cotangent, out_weight, values, gate_input, conv_out, filter_taps):
    block_rows, channels = values.shape
    count = lax.axis_size("seq")
    parts = lax.axis_size("fsdp")
    rows = out_weight.shape[1]
    features = rows * count
    per = channels // count
    forward, value_back, filter_back = (jnp.asarray(t) for t in make_tables(block_rows))
    cot, weight, vals = cotangent.T, out_weight.T, values.T
    gate, conv = gate_input.T, conv_out.T
    shape = jax.ShapeDtypeStruct
    chips = count // 2
    same_core = [list(range(core, count, 2)) for core in range(2)]
    exchange = lambda x: lax.all_to_all(x, "seq", 0, 0, axis_index_groups=same_core)
    swap = lambda x: lax.ppermute(x, "seq", [(i, i ^ 1) for i in range(count)])
    cross = lambda x, mask: lax.ppermute(x, "fsdp", [(i, i ^ mask) for i in range(parts)])
    half = rows // 2
    wide = [pltpu.VMEM((channels + 8, block_rows), F32)]

    sent = call(
        functools.partial(pack_body, chips, per),
        shape((chips, rows + half + 16, block_rows), BF16), wide, 1000, weight, vals, room=60 * 1024 * 1024,
    )
    got = exchange(sent)
    masks = tuple(range(parts))
    near = jnp.stack([cot if mask == 0 else cross(cot, mask) for mask in masks[: parts // 2]])
    far = cross(near, parts // 2)
    got, far = lax.optimization_barrier((got, far))
    other = swap(got)
    grad_gate, mine = call(
        functools.partial(front_body, count, per, masks),
        (shape((channels, block_rows), BF16), shape((chips, 16, block_rows), BF16)),
        [pltpu.VMEM((features, 2 * block_rows), BF16), *wide],
        2 * features * channels * block_rows, got, other, near, far, gate, conv,
    )
    terms = shape((chips, rows + half, block_rows), BF16)
    keep, give = call(
        functools.partial(terms_body, count, masks),
        (terms, terms), [], 2 * features * channels * block_rows, near, far, gate, conv,
    )
    joined = call(join_body, terms, [], chips * (rows + half) * block_rows, keep, swap(give))
    mine = exchange(mine)
    theirs = swap(mine)
    length = filter_taps.shape[1]
    inside, outside = pl.BlockSpec(memory_space=pltpu.VMEM), pl.BlockSpec(memory_space=pltpu.HBM)
    ordered = pltpu.VMEM((count * 8, block_rows), BF16)
    forms = call(
        functools.partial(spectra_body, per), shape((10, count * 8, block_rows), F32),
        [pltpu.VMEM((16, length), BF16), ordered, pltpu.SemaphoreType.DMA],
        6 * count * 8 * block_rows * 2 * block_rows, got, other, filter_taps, forward, value_back, filter_back,
        in_specs=[inside, inside, outside, inside, inside, inside],
    )
    result = shape((chips, 16, block_rows), BF16)
    stay, leave = call(
        functools.partial(mix_body, count), (result, result),
        [
            ordered,
            pltpu.VMEM((count * 8, 2 * block_rows), F32),
            pltpu.VMEM((count * 8, 2 * block_rows), F32),
            pltpu.VMEM((count * 8 + 8, 2 * block_rows), F32),
        ],
        8 * count * 8 * block_rows * 2 * block_rows, mine, theirs, forms,
    )
    both = call(
        last_body, shape((chips, 32 + rows + half, block_rows), BF16), [], 1000, stay, swap(leave), joined
    )
    grad_value, grad_filter, grad_weight = call(
        functools.partial(finish_body, per),
        (shape((channels, block_rows), BF16), shape((channels, block_rows), F32), shape((rows, channels), F32)),
        wide, 1000, exchange(both),
    )
    return (grad_value.T, grad_gate.T, grad_filter.T, grad_weight.T)


def solution(mesh):
    in_specs = (
        P("seq", "fsdp"),
        P("fsdp", "seq"),
        P("seq", "fsdp"),
        P("seq", "fsdp"),
        P("seq", "fsdp"),
        P("fsdp", None),
    )
    out_specs = (P("seq", "fsdp"), P("seq", "fsdp"), P("seq", "fsdp"), P("fsdp", "seq"))
    return jax.shard_map(body, mesh=mesh, in_specs=in_specs, out_specs=out_specs, check_vma=False)
```

```python
import functools

import jax
import jax.numpy as jnp
import numpy as np
from jax import lax
from jax.experimental import pallas as pl
from jax.experimental.pallas import tpu as pltpu
from jax.sharding import PartitionSpec as P

F32 = jnp.float32
BF16 = jnp.bfloat16


def make_tables(block_rows):
    n, period = block_rows, 2 * block_rows
    freq = np.arange(n)
    pos = np.arange(period)
    angle = 2.0 * np.pi * ((freq[:, None] * pos[None, :]) % period) / period
    cos = np.cos(angle)
    sin = np.sin(angle)
    sign = (1.0 - 2.0 * (freq % 2))[:, None]
    alt = (1.0 - 2.0 * (pos % 2))[None, :]
    narrow = lambda a: np.asarray(a, np.float32).astype(jnp.bfloat16)
    fwd_im = np.where(freq[:, None] == 0, alt, -sin)
    forward = np.concatenate([narrow(cos), narrow(fwd_im)], axis=0).T
    both = np.where(freq[:, None] == 0, 1.0, 2.0)
    back_cos = narrow(sign * cos / period).astype(np.float32) * both
    back_sin = narrow(-sign * sin / period).astype(np.float32) * both
    last = narrow(alt / period).astype(np.float32)
    first = freq[:, None] == 0
    value_back = np.concatenate([back_cos, np.where(first, last, -back_sin)], axis=0)[:, :n]
    filter_back = np.concatenate([back_cos, np.where(first, last, back_sin)], axis=0)
    return (
        np.ascontiguousarray(forward),
        np.ascontiguousarray(narrow(value_back)),
        np.ascontiguousarray(narrow(filter_back)),
    )


def dot(left, right, dims):
    return lax.dot_general(left, right, (dims, ((), ())), preferred_element_type=F32)


def call(body, out_shape, scratch, cost, *args, room=32 * 1024 * 1024, **specs):
    return pl.pallas_call(
        body,
        out_shape=out_shape,
        scratch_shapes=scratch,
        **specs,
        cost_estimate=pl.CostEstimate(flops=cost, bytes_accessed=1000000, transcendentals=0),
        compiler_params=pltpu.CompilerParams(vmem_limit_bytes=room),
    )(*args)


def window_start(per, length, size):
    return pl.multiple_of(jnp.minimum(lax.axis_index("seq") * per // 8 * 8, length - size), 8)


def pack_body(chips, per, flip, w_hbm, v_hbm, taps_ref, out_ref, window_ref, w_ref, v_ref, wide, sems):
    source = taps_ref.at[pl.ds(window_start(per, taps_ref.shape[0], window_ref.shape[0]), window_ref.shape[0])]
    pairs = ((w_hbm, w_ref), (v_hbm, v_ref), (source, window_ref))
    copies = [pltpu.make_async_copy(*pair, sems.at[i]) for i, pair in enumerate(pairs)]
    for copy in copies:
        copy.start()
    copies[0].wait()
    copies[1].wait()
    rows, channels = w_ref.shape
    half = rows // 2
    lanes = v_ref.shape[1]
    main = w_ref[:, :lanes]
    w = w_ref[...].astype(F32)
    side = jnp.concatenate([w[:half, lanes:], w[half:, lanes:]], axis=1).astype(BF16)
    wide[channels:, :] = jnp.zeros((wide.shape[0] - channels, lanes), F32)
    wide[:channels, :] = v_ref[...].astype(F32)
    for chip in range(chips):
        place = chip ^ flip
        out_ref[place, :rows, :] = main
        out_ref[place, rows : rows + half, :] = side
        for core in range(2):
            at = rows + half + 8 * core
            begin = per * (2 * chip + core)
            out_ref[place, at : at + 8, :] = wide[begin : begin + 8, :].astype(BF16)
    copies[2].wait()


def terms_body(groups, masks, flip, *refs):
    *pieces, g_ref, o_ref, keep_ref, send_ref = refs
    lanes = g_ref.shape[1]
    channels = g_ref.shape[0]
    here = lax.axis_index("fsdp")
    core = lax.rem(lax.axis_index("seq"), 2)
    share = groups // len(masks)
    rows = channels // share
    half = rows // 2
    gated = (g_ref[...].astype(F32) * o_ref[...].astype(F32)).astype(BF16)
    rest = gated[lanes:]
    zero = jnp.zeros_like(rest)
    lower = jnp.concatenate([rest, zero], axis=0)
    upper = jnp.concatenate([zero, rest], axis=0)
    blocks = len(masks) // len(pieces)
    for part, source in enumerate(pieces):
        f = source[...].reshape(blocks * channels, lanes)
        main = dot(f, gated[:lanes], ((1,), (1,))).astype(BF16).reshape(blocks * share, rows, lanes)
        f3 = f.reshape(blocks * share, rows, lanes)
        low = f3[:, :half].reshape(blocks * share * half, lanes)
        high = f3[:, half:].reshape(blocks * share * half, lanes)
        side = dot(low, lower, ((1,), (1,))) + dot(high, upper, ((1,), (1,)))
        side = side.astype(BF16).reshape(blocks * share, half, lanes)

        def put(*refs):
            for i in range(blocks):
                first = jnp.bitwise_xor(here, masks[part * blocks + i]) * (share // 2)
                for q in range(share):
                    place = jnp.bitwise_xor(first + q // 2, flip)
                    refs[q % 2][place, :rows, :] = main[i * share + q]
                    refs[q % 2][place, rows:, :] = side[i * share + q]

        @pl.when(core == 0)
        def _():
            put(keep_ref, send_ref)

        @pl.when(core == 1)
        def _():
            put(send_ref, keep_ref)


def front_body(groups, per, masks, flip, flip_out, own_ref, other_ref, *refs):
    *pieces, g_ref, o_ref, gate_ref, out_ref, weight, wide = refs
    lanes = g_ref.shape[1]
    channels = g_ref.shape[0]
    here = lax.axis_index("fsdp")
    core = lax.rem(lax.axis_index("seq"), 2)
    share = groups // len(masks)
    rows = channels // share
    half = rows // 2
    for source, which in ((own_ref, core), (other_ref, 1 - core)):
        for slot in range(len(masks)):
            for q in range(share // 2):
                chip = jnp.bitwise_xor(jnp.bitwise_xor(here, masks[slot]) * (share // 2) + q, flip)
                at = pl.multiple_of(rows * (slot * share + 2 * q + which), 8)
                weight[pl.ds(at, rows), :lanes] = source[chip, :rows, :]
                side = source[chip, rows : rows + half, :]
                weight[pl.ds(at, half), lanes:] = side
                turned = jnp.concatenate([side[:, lanes // 2 :], side[:, : lanes // 2]], axis=1)
                weight[pl.ds(at + half, half), lanes:] = turned
    size = groups * rows // len(pieces)
    mixed = 0.0
    for part, source in enumerate(pieces):
        piece = weight[part * size : (part + 1) * size]
        mixed = mixed + dot(piece, source[...].reshape(size, lanes), ((0,), (0,)))
    mixed = mixed[:channels]
    gate_ref[...] = (mixed * o_ref[...].astype(F32)).astype(BF16)
    wide[channels:, :] = jnp.zeros((wide.shape[0] - channels, lanes), F32)
    wide[:channels, :] = mixed * g_ref[...].astype(F32)
    for chip in range(groups // 2):
        for c in range(2):
            begin = per * (2 * chip + c)
            out_ref[chip ^ flip_out, 8 * c : 8 * c + 8, :] = wide[begin : begin + 8, :].astype(BF16)


def in_order(own_ref, other_ref, row, flip, blocks):
    core = lax.rem(lax.axis_index("seq"), 2)
    at = pl.multiple_of(row + 8 * core, 8)
    for chip in range(own_ref.shape[0]):
        blocks[pl.ds(pl.multiple_of(16 * chip + 8 * core, 8), 8), :] = own_ref[chip ^ flip, pl.ds(at, 8), :]
        blocks[pl.ds(pl.multiple_of(16 * chip + 8 * (1 - core), 8), 8), :] = other_ref[chip ^ flip, pl.ds(at, 8), :]


def join_body(keep_ref, came_ref, out_ref):
    out_ref[...] = (keep_ref[...].astype(F32) + came_ref[...].astype(F32)).astype(BF16)


def spectra_body(
    per, flip, length, own_ref, other_ref, near_ref, table_ref, vback_ref, fback_ref, out_ref, tables_ref, blocks
):
    groups = 2 * own_ref.shape[0]
    lanes = own_ref.shape[2]
    window = near_ref.shape[0]
    start = lax.axis_index("seq") * per - window_start(per, length, window)
    rows = groups * 8
    table = table_ref[...]
    in_order(own_ref, other_ref, own_ref.shape[1] - 16, flip, blocks)
    val = dot(blocks[...], table[:lanes], ((1,), (0,)))
    out_ref[2] = val[:, :lanes]
    out_ref[3] = val[:, lanes:]
    own = pltpu.roll(near_ref[...].astype(F32), window - start, 0)[:8].astype(BF16)
    taps = jnp.concatenate([own[:, i * lanes : (i + 1) * lanes] for i in range(groups)], axis=0)
    upper = dot(taps, table[lanes:], ((1,), (0,)))
    lower = dot(taps, table[:lanes], ((1,), (0,)))
    lower = jnp.concatenate([jnp.zeros((8, 2 * lanes), F32), lower[: rows - 8]], axis=0)
    spec = upper + lower
    out_ref[0] = spec[:, :lanes]
    out_ref[1] = spec[:, lanes:]
    tables_ref[0, :lanes] = table[:lanes, :lanes]
    tables_ref[0, lanes:] = table[:lanes, lanes:]
    tables_ref[1] = vback_ref[...]
    tables_ref[2] = fback_ref[:, :lanes]
    tables_ref[3] = fback_ref[:, lanes:]


def mix_body(count, flip, flip_out, own_ref, other_ref, forms_ref, tables_ref, keep_ref, send_ref, blocks, conv, vmix, fmix):
    lanes = own_ref.shape[2]
    rows = count * 8
    in_order(own_ref, other_ref, 0, flip, blocks)
    g = blocks[...]
    conv[:, :lanes] = dot(g, tables_ref[0, :lanes], ((1,), (0,)))
    conv[:, lanes:] = dot(g, tables_ref[0, lanes:], ((1,), (0,)))
    tile = 8
    first = lax.broadcasted_iota(jnp.int32, (8, lanes), 1) == 0
    for base in range(0, count, tile):
        zero = jnp.zeros((8, lanes), F32)
        acc = [[zero] * 4 for _ in range(tile)]
        for shift in range(count - base):
            at = pl.ds(8 * shift, 8)
            tr, ti, vr, vi = (forms_ref[plane, at] for plane in range(4))
            tb, td = jnp.where(first, 0.0, ti), jnp.where(first, ti, -tr)
            vb, vd = jnp.where(first, 0.0, vi), jnp.where(first, vi, vr)
            for r in range(min(tile, count - base - shift)):
                place = pl.ds(8 * (base + r + shift), 8)
                cr = conv[place, :lanes]
                ci = conv[place, lanes:]
                a = acc[r]
                acc[r] = [
                    a[0] + cr * tr + ci * tb,
                    a[1] + cr * tb + ci * td,
                    a[2] + cr * vr + ci * vb,
                    a[3] + ci * vd - cr * vb,
                ]
        for r in range(tile):
            place = pl.ds(8 * (base + r), 8)
            vmix[place, :lanes] = acc[r][0]
            vmix[place, lanes:] = acc[r][1]
            fmix[place, :lanes] = acc[r][2]
            fmix[place, lanes:] = acc[r][3]
    fmix[rows:, :] = jnp.zeros((8, 2 * lanes), F32)
    value = dot(vmix[...].astype(BF16), tables_ref[1], ((1,), (0,)))
    late = dot(fmix[:rows].astype(BF16), tables_ref[3], ((1,), (0,)))
    early = dot(fmix[8:].astype(BF16), tables_ref[2], ((1,), (0,)))
    value = value.astype(BF16).reshape(count, 8, lanes)
    lags = (late + early).astype(BF16).reshape(count, 8, lanes)

    def put(*refs):
        for i in range(count):
            refs[i % 2][(i // 2) ^ flip_out, :8, :] = value[i]
            refs[i % 2][(i // 2) ^ flip_out, 8:, :] = lags[i]

    core = lax.rem(lax.axis_index("seq"), 2)

    @pl.when(core == 0)
    def _():
        put(keep_ref, send_ref)

    @pl.when(core == 1)
    def _():
        put(send_ref, keep_ref)


def last_body(keep_ref, came_ref, joined_ref, out_ref):
    core = lax.rem(lax.axis_index("seq"), 2)
    out_ref[:, pl.ds(pl.multiple_of(16 * core, 8), 16), :] = keep_ref[...]
    out_ref[:, pl.ds(pl.multiple_of(16 * (1 - core), 8), 16), :] = came_ref[...]
    out_ref[:, 32:, :] = joined_ref[...]


def finish_body(per, flip, in_ref, value_ref, filter_ref, weight_ref, wide):
    chips, packed, lanes = in_ref.shape
    channels = value_ref.shape[0]
    for row, target in ((0, value_ref), (8, filter_ref)):
        for chip in range(chips):
            for c in range(2):
                at = per * (2 * chip + c)
                wide[at : at + 8, :] = in_ref[chip ^ flip, row + 16 * c : row + 16 * c + 8, :].astype(F32)
        target[...] = wide[:channels, :].astype(target.dtype)
    rows = weight_ref.shape[0]
    half = rows // 2
    total = in_ref[0, 32:, :].astype(F32)
    for chip in range(1, chips):
        total = total + in_ref[chip, 32:, :].astype(F32)
    weight_ref[:, :lanes] = total[:rows]
    rest = channels - lanes
    weight_ref[:half, lanes:] = total[rows:, :rest]
    weight_ref[half:, lanes:] = total[rows:, rest:]


def body(cotangent, out_weight, values, gate_input, conv_out, filter_taps):
    block_rows, channels = values.shape
    count = lax.axis_size("seq")
    parts = lax.axis_size("fsdp")
    rows = out_weight.shape[1]
    features = rows * count
    per = channels // count
    forward, value_back, filter_back = (jnp.asarray(t) for t in make_tables(block_rows))
    cot, weight, vals = cotangent.T, out_weight.T, values.T
    gate, conv = gate_input.T, conv_out.T
    shape = jax.ShapeDtypeStruct
    chips = count // 2
    far_chip = chips // 2 + chips // 4
    flips = (far_chip, chips // 2, chips // 2)

    def exchange(x, flip):
        same_core = [[2 * (place ^ flip) + core for place in range(chips)] for core in range(2)]
        return lax.all_to_all(x, "seq", 0, 0, axis_index_groups=same_core)

    swap = lambda x: lax.ppermute(x, "seq", [(i, i ^ 1) for i in range(count)])
    cross = lambda x, mask: lax.ppermute(x, "fsdp", [(i, i ^ mask) for i in range(parts)])
    half = rows // 2
    wide = [pltpu.VMEM((channels + 8, block_rows), F32)]

    inside, outside = pl.BlockSpec(memory_space=pltpu.VMEM), pl.BlockSpec(memory_space=pltpu.HBM)
    sent, window = call(
        functools.partial(pack_body, chips, per, flips[0]),
        (shape((chips, rows + half + 16, block_rows), BF16), shape((16, filter_taps.shape[1]), BF16)),
        [pltpu.VMEM(weight.shape, BF16), pltpu.VMEM(vals.shape, BF16), *wide, pltpu.SemaphoreType.DMA((3,))],
        1000, weight, vals, filter_taps, room=60 * 1024 * 1024, in_specs=[outside] * 3, out_specs=(inside, inside),
    )
    across = cross(cot, parts // 2)
    sent, across = lax.optimization_barrier((sent, across))
    got = exchange(sent, flips[0])
    pair = jnp.stack([cot, across])
    pieces = [pair, cross(pair, 1), cross(pair, 3), cross(pair, 2)]
    masks = (0, 4, 1, 5, 3, 7, 2, 6)
    got, *pieces = lax.optimization_barrier((got, *pieces))
    other = swap(got)
    grad_gate, mine = call(
        functools.partial(front_body, count, per, masks, *flips[:2]),
        (shape((channels, block_rows), BF16), shape((chips, 16, block_rows), BF16)),
        [pltpu.VMEM((features, 2 * block_rows), BF16), *wide],
        2 * features * channels * block_rows, got, other, *pieces, gate, conv,
    )
    terms = shape((chips, rows + half, block_rows), BF16)
    keep, give = call(
        functools.partial(terms_body, count, masks, flips[2]),
        (terms, terms), [], 2 * features * channels * block_rows, *pieces, gate, conv,
    )
    joined = call(join_body, terms, [], chips * (rows + half) * block_rows, keep, swap(give))
    mine = exchange(mine, flips[1])
    ordered = pltpu.VMEM((count * 8, block_rows), BF16)
    forms, tables = call(
        functools.partial(spectra_body, per, flips[0], channels),
        (shape((4, count * 8, block_rows), F32), shape((4, 2 * block_rows, block_rows), BF16)), [ordered],
        6 * count * 8 * block_rows * 2 * block_rows, got, other, window, forward, value_back, filter_back,
    )
    theirs = swap(mine)
    result = shape((chips, 16, block_rows), BF16)
    stay, leave = call(
        functools.partial(mix_body, count, *flips[1:]), (result, result),
        [
            ordered,
            pltpu.VMEM((count * 8, 2 * block_rows), F32),
            pltpu.VMEM((count * 8, 2 * block_rows), F32),
            pltpu.VMEM((count * 8 + 8, 2 * block_rows), F32),
        ],
        8 * count * 8 * block_rows * 2 * block_rows, mine, theirs, forms, tables,
    )
    both = call(
        last_body, shape((chips, 32 + rows + half, block_rows), BF16), [], 1000, stay, swap(leave), joined
    )
    grad_value, grad_filter, grad_weight = call(
        functools.partial(finish_body, per, flips[2]),
        (shape((channels, block_rows), BF16), shape((channels, block_rows), F32), shape((rows, channels), F32)),
        wide, 1000, exchange(both, flips[2]),
    )
    return (grad_value.T, grad_gate.T, grad_filter.T, grad_weight.T)


def solution(mesh):
    in_specs = (
        P("seq", "fsdp"),
        P("fsdp", "seq"),
        P("seq", "fsdp"),
        P("seq", "fsdp"),
        P("seq", "fsdp"),
        P("fsdp", None),
    )
    out_specs = (P("seq", "fsdp"), P("seq", "fsdp"), P("seq", "fsdp"), P("fsdp", "seq"))
    return jax.shard_map(body, mesh=mesh, in_specs=in_specs, out_specs=out_specs, check_vma=False)
```

```python
import functools

import jax
import jax.numpy as jnp
import numpy as np
from jax import lax
from jax.experimental import pallas as pl
from jax.experimental.pallas import tpu as pltpu
from jax.sharding import PartitionSpec as P

F32 = jnp.float32
BF16 = jnp.bfloat16


def make_tables(block_rows):
    n, period = block_rows, 2 * block_rows
    freq = np.arange(n)
    pos = np.arange(period)
    angle = 2.0 * np.pi * ((freq[:, None] * pos[None, :]) % period) / period
    cos = np.cos(angle)
    sin = np.sin(angle)
    sign = (1.0 - 2.0 * (freq % 2))[:, None]
    alt = (1.0 - 2.0 * (pos % 2))[None, :]
    narrow = lambda a: np.asarray(a, np.float32).astype(jnp.bfloat16)
    fwd_im = np.where(freq[:, None] == 0, alt, -sin)
    forward = np.concatenate([narrow(cos), narrow(fwd_im)], axis=0).T
    both = np.where(freq[:, None] == 0, 1.0, 2.0)
    back_cos = narrow(sign * cos / period).astype(np.float32) * both
    back_sin = narrow(-sign * sin / period).astype(np.float32) * both
    last = narrow(alt / period).astype(np.float32)
    first = freq[:, None] == 0
    value_back = np.concatenate([back_cos, np.where(first, last, -back_sin)], axis=0)[:, :n]
    filter_back = np.concatenate([back_cos, np.where(first, last, back_sin)], axis=0)
    return (
        np.ascontiguousarray(forward),
        np.ascontiguousarray(narrow(value_back)),
        np.ascontiguousarray(narrow(filter_back)),
    )


def dot(left, right, dims):
    return lax.dot_general(left, right, (dims, ((), ())), preferred_element_type=F32)


def call(body, out_shape, scratch, cost, *args, room=32 * 1024 * 1024, **specs):
    return pl.pallas_call(
        body,
        out_shape=out_shape,
        scratch_shapes=scratch,
        **specs,
        cost_estimate=pl.CostEstimate(flops=cost, bytes_accessed=1000000, transcendentals=0),
        compiler_params=pltpu.CompilerParams(vmem_limit_bytes=room),
    )(*args)


def window_start(per, length, size):
    return pl.multiple_of(jnp.minimum(lax.axis_index("seq") * per // 8 * 8, length - size), 8)


def pack_body(chips, per, flip, w_hbm, v_hbm, taps_ref, out_ref, window_ref, w_ref, v_ref, wide, sems):
    source = taps_ref.at[pl.ds(window_start(per, taps_ref.shape[0], window_ref.shape[0]), window_ref.shape[0])]
    pairs = ((w_hbm, w_ref), (v_hbm, v_ref), (source, window_ref))
    copies = [pltpu.make_async_copy(*pair, sems.at[i]) for i, pair in enumerate(pairs)]
    for copy in copies:
        copy.start()
    copies[0].wait()
    copies[1].wait()
    rows, channels = w_ref.shape
    half = rows // 2
    lanes = v_ref.shape[1]
    main = w_ref[:, :lanes]
    w = w_ref[...].astype(F32)
    side = jnp.concatenate([w[:half, lanes:], w[half:, lanes:]], axis=1).astype(BF16)
    wide[channels:, :] = jnp.zeros((wide.shape[0] - channels, lanes), F32)
    wide[:channels, :] = v_ref[...].astype(F32)
    for chip in range(chips):
        place = chip ^ flip
        out_ref[place, :rows, :] = main
        out_ref[place, rows : rows + half, :] = side
        for core in range(2):
            at = rows + half + 8 * core
            begin = per * (2 * chip + core)
            out_ref[place, at : at + 8, :] = wide[begin : begin + 8, :].astype(BF16)
    copies[2].wait()


def terms_body(groups, masks, flip, *refs):
    *pieces, g_ref, o_ref, keep_ref, send_ref = refs
    lanes = g_ref.shape[1]
    channels = g_ref.shape[0]
    here = lax.axis_index("fsdp")
    core = lax.rem(lax.axis_index("seq"), 2)
    late = lax.axis_index("seq") // (groups // 2)
    share = groups // len(masks)
    rows = channels // share
    half = rows // 2
    cut = keep_ref.shape[2]
    gated = (g_ref[...].astype(F32) * o_ref[...].astype(F32)).astype(BF16)
    rest = gated[lanes:]
    zero = jnp.zeros_like(rest)
    lower = jnp.concatenate([rest, zero], axis=0)
    upper = jnp.concatenate([zero, rest], axis=0)
    blocks = len(masks) // len(pieces)
    for part, source in enumerate(pieces):
        f = source[...].reshape(blocks * channels, lanes)
        main = dot(f, gated[:lanes], ((1,), (1,))).astype(BF16).reshape(blocks * share, rows, lanes)
        f3 = f.reshape(blocks * share, rows, lanes)
        low = f3[:, :half].reshape(blocks * share * half, lanes)
        high = f3[:, half:].reshape(blocks * share * half, lanes)
        side = dot(low, lower, ((1,), (1,))) + dot(high, upper, ((1,), (1,)))
        side = side.astype(BF16).reshape(blocks * share, half, lanes)

        def put(*refs):
            for i in range(blocks):
                first = jnp.bitwise_xor(here, masks[part * blocks + i]) * (share // 2)
                for q in range(share):
                    ref = refs[q % 2]
                    place = jnp.bitwise_xor(first + q // 2, flip)
                    ref[late, place] = main[i * share + q, :cut]
                    ref[1 - late, place, : rows - cut, :] = main[i * share + q, cut:]
                    ref[1 - late, place, rows - cut : rows - cut + half, :] = side[i * share + q]
                    ref[1 - late, place, rows - cut + half :, :] = jnp.zeros((2 * cut - rows - half, lanes), BF16)

        @pl.when(core == 0)
        def _():
            put(keep_ref, send_ref)

        @pl.when(core == 1)
        def _():
            put(send_ref, keep_ref)


def front_body(groups, per, masks, flip, flip_out, own_ref, other_ref, *refs):
    *pieces, g_ref, o_ref, gate_ref, out_ref, weight, wide = refs
    lanes = g_ref.shape[1]
    channels = g_ref.shape[0]
    here = lax.axis_index("fsdp")
    core = lax.rem(lax.axis_index("seq"), 2)
    share = groups // len(masks)
    rows = channels // share
    half = rows // 2
    for source, which in ((own_ref, core), (other_ref, 1 - core)):
        for slot in range(len(masks)):
            for q in range(share // 2):
                chip = jnp.bitwise_xor(jnp.bitwise_xor(here, masks[slot]) * (share // 2) + q, flip)
                at = pl.multiple_of(rows * (slot * share + 2 * q + which), 8)
                weight[pl.ds(at, rows), :lanes] = source[chip, :rows, :]
                side = source[chip, rows : rows + half, :]
                weight[pl.ds(at, half), lanes:] = side
                turned = jnp.concatenate([side[:, lanes // 2 :], side[:, : lanes // 2]], axis=1)
                weight[pl.ds(at + half, half), lanes:] = turned
    size = groups * rows // len(pieces)
    mixed = 0.0
    for part, source in enumerate(pieces):
        piece = weight[part * size : (part + 1) * size]
        mixed = mixed + dot(piece, source[...].reshape(size, lanes), ((0,), (0,)))
    mixed = mixed[:channels]
    gate_ref[...] = (mixed * o_ref[...].astype(F32)).astype(BF16)
    wide[channels:, :] = jnp.zeros((wide.shape[0] - channels, lanes), F32)
    wide[:channels, :] = mixed * g_ref[...].astype(F32)
    for chip in range(groups // 2):
        for c in range(2):
            begin = per * (2 * chip + c)
            out_ref[chip ^ flip_out, 8 * c : 8 * c + 8, :] = wide[begin : begin + 8, :].astype(BF16)


def in_order(own_ref, other_ref, row, flip, blocks):
    core = lax.rem(lax.axis_index("seq"), 2)
    at = pl.multiple_of(row + 8 * core, 8)
    for chip in range(own_ref.shape[0]):
        blocks[pl.ds(pl.multiple_of(16 * chip + 8 * core, 8), 8), :] = own_ref[chip ^ flip, pl.ds(at, 8), :]
        blocks[pl.ds(pl.multiple_of(16 * chip + 8 * (1 - core), 8), 8), :] = other_ref[chip ^ flip, pl.ds(at, 8), :]


def join_body(keep_ref, came_ref, stay_ref, leave_ref):
    stay_ref[...] = (keep_ref[0].astype(F32) + came_ref[0].astype(F32)).astype(BF16)
    leave_ref[...] = (keep_ref[1].astype(F32) + came_ref[1].astype(F32)).astype(BF16)


def spectra_body(
    per, flip, length, own_ref, other_ref, near_ref, table_ref, vback_ref, fback_ref, out_ref, tables_ref, blocks
):
    groups = 2 * own_ref.shape[0]
    lanes = own_ref.shape[2]
    window = near_ref.shape[0]
    start = lax.axis_index("seq") * per - window_start(per, length, window)
    rows = groups * 8
    table = table_ref[...]
    in_order(own_ref, other_ref, own_ref.shape[1] - 16, flip, blocks)
    val = dot(blocks[...], table[:lanes], ((1,), (0,)))
    out_ref[2] = val[:, :lanes]
    out_ref[3] = val[:, lanes:]
    own = pltpu.roll(near_ref[...].astype(F32), window - start, 0)[:8].astype(BF16)
    taps = jnp.concatenate([own[:, i * lanes : (i + 1) * lanes] for i in range(groups)], axis=0)
    upper = dot(taps, table[lanes:], ((1,), (0,)))
    lower = dot(taps, table[:lanes], ((1,), (0,)))
    lower = jnp.concatenate([jnp.zeros((8, 2 * lanes), F32), lower[: rows - 8]], axis=0)
    spec = upper + lower
    out_ref[0] = spec[:, :lanes]
    out_ref[1] = spec[:, lanes:]
    tables_ref[0, :lanes] = table[:lanes, :lanes]
    tables_ref[0, lanes:] = table[:lanes, lanes:]
    tables_ref[1] = vback_ref[...]
    tables_ref[2] = fback_ref[:, :lanes]
    tables_ref[3] = fback_ref[:, lanes:]


def mix_body(count, flip, flip_out, own_ref, other_ref, forms_ref, tables_ref, keep_ref, send_ref, blocks, conv, vmix, fmix):
    lanes = own_ref.shape[2]
    rows = count * 8
    in_order(own_ref, other_ref, 0, flip, blocks)
    g = blocks[...]
    conv[:, :lanes] = dot(g, tables_ref[0, :lanes], ((1,), (0,)))
    conv[:, lanes:] = dot(g, tables_ref[0, lanes:], ((1,), (0,)))
    tile = 8
    first = lax.broadcasted_iota(jnp.int32, (8, lanes), 1) == 0
    for base in range(0, count, tile):
        zero = jnp.zeros((8, lanes), F32)
        acc = [[zero] * 4 for _ in range(tile)]
        for shift in range(count - base):
            at = pl.ds(8 * shift, 8)
            tr, ti, vr, vi = (forms_ref[plane, at] for plane in range(4))
            tb, td = jnp.where(first, 0.0, ti), jnp.where(first, ti, -tr)
            vb, vd = jnp.where(first, 0.0, vi), jnp.where(first, vi, vr)
            for r in range(min(tile, count - base - shift)):
                place = pl.ds(8 * (base + r + shift), 8)
                cr = conv[place, :lanes]
                ci = conv[place, lanes:]
                a = acc[r]
                acc[r] = [
                    a[0] + cr * tr + ci * tb,
                    a[1] + cr * tb + ci * td,
                    a[2] + cr * vr + ci * vb,
                    a[3] + ci * vd - cr * vb,
                ]
        for r in range(tile):
            place = pl.ds(8 * (base + r), 8)
            vmix[place, :lanes] = acc[r][0]
            vmix[place, lanes:] = acc[r][1]
            fmix[place, :lanes] = acc[r][2]
            fmix[place, lanes:] = acc[r][3]
    fmix[rows:, :] = jnp.zeros((8, 2 * lanes), F32)
    value = dot(vmix[...].astype(BF16), tables_ref[1], ((1,), (0,)))
    late = dot(fmix[:rows].astype(BF16), tables_ref[3], ((1,), (0,)))
    early = dot(fmix[8:].astype(BF16), tables_ref[2], ((1,), (0,)))
    value = value.astype(BF16).reshape(count, 8, lanes)
    lags = (late + early).astype(BF16).reshape(count, 8, lanes)

    def put(*refs):
        for i in range(count):
            refs[i % 2][(i // 2) ^ flip_out, :8, :] = value[i]
            refs[i % 2][(i // 2) ^ flip_out, 8:, :] = lags[i]

    core = lax.rem(lax.axis_index("seq"), 2)

    @pl.when(core == 0)
    def _():
        put(keep_ref, send_ref)

    @pl.when(core == 1)
    def _():
        put(send_ref, keep_ref)


def last_body(keep_ref, came_ref, terms_ref, more_ref, out_ref):
    core = lax.rem(lax.axis_index("seq"), 2)
    out_ref[:, pl.ds(pl.multiple_of(16 * core, 8), 16), :] = keep_ref[...]
    out_ref[:, pl.ds(pl.multiple_of(16 * (1 - core), 8), 16), :] = came_ref[...]
    out_ref[:, 32:, :] = (terms_ref[...].astype(F32) + more_ref[...].astype(F32)).astype(BF16)


def finish_body(per, flip, in_ref, value_ref, filter_ref, weight_ref, wide):
    chips, packed, lanes = in_ref.shape
    channels = value_ref.shape[0]
    for row, target in ((0, value_ref), (8, filter_ref)):
        for chip in range(chips):
            for c in range(2):
                at = per * (2 * chip + c)
                wide[at : at + 8, :] = in_ref[chip ^ flip, row + 16 * c : row + 16 * c + 8, :].astype(F32)
        target[...] = wide[:channels, :].astype(target.dtype)
    rows = weight_ref.shape[0]
    half = rows // 2
    first, second = in_ref[0 ^ flip, 32:, :].astype(F32), in_ref[(chips // 2) ^ flip, 32:, :].astype(F32)
    for chip in range(1, chips // 2):
        first = first + in_ref[chip ^ flip, 32:, :].astype(F32)
        second = second + in_ref[(chip + chips // 2) ^ flip, 32:, :].astype(F32)
    cut = packed - 32
    weight_ref[:cut, :lanes] = first
    weight_ref[cut:, :lanes] = second[: rows - cut]
    side = second[rows - cut : rows - cut + half]
    rest = channels - lanes
    weight_ref[:half, lanes:] = side[:, :rest]
    weight_ref[half:, lanes:] = side[:, rest:]


def body(cotangent, out_weight, values, gate_input, conv_out, filter_taps):
    block_rows, channels = values.shape
    count = lax.axis_size("seq")
    parts = lax.axis_size("fsdp")
    rows = out_weight.shape[1]
    features = rows * count
    per = channels // count
    forward, value_back, filter_back = (jnp.asarray(t) for t in make_tables(block_rows))
    cot, weight, vals = cotangent.T, out_weight.T, values.T
    gate, conv = gate_input.T, conv_out.T
    shape = jax.ShapeDtypeStruct
    chips = count // 2
    far_chip = chips // 2 + chips // 4
    flips = (far_chip, chips // 2, chips // 2)

    def exchange(x, flip):
        same_core = [[2 * (place ^ flip) + core for place in range(chips)] for core in range(2)]
        return lax.all_to_all(x, "seq", 0, 0, axis_index_groups=same_core)

    swap = lambda x: lax.ppermute(x, "seq", [(i, i ^ 1) for i in range(count)])
    cross = lambda x, mask: lax.ppermute(x, "fsdp", [(i, i ^ mask) for i in range(parts)])
    half = rows // 2
    wide = [pltpu.VMEM((channels + 8, block_rows), F32)]

    inside, outside = pl.BlockSpec(memory_space=pltpu.VMEM), pl.BlockSpec(memory_space=pltpu.HBM)
    sent, window = call(
        functools.partial(pack_body, chips, per, flips[0]),
        (shape((chips, rows + half + 16, block_rows), BF16), shape((16, filter_taps.shape[1]), BF16)),
        [pltpu.VMEM(weight.shape, BF16), pltpu.VMEM(vals.shape, BF16), *wide, pltpu.SemaphoreType.DMA((3,))],
        1000, weight, vals, filter_taps, room=60 * 1024 * 1024, in_specs=[outside] * 3, out_specs=(inside, inside),
    )
    across = cross(cot, parts // 2)
    sent, across = lax.optimization_barrier((sent, across))
    got = exchange(sent, flips[0])
    pair = jnp.stack([cot, across])
    pieces = [pair, cross(pair, 1), cross(pair, 3), cross(pair, 2)]
    masks = (0, 4, 1, 5, 3, 7, 2, 6)
    got, *pieces = lax.optimization_barrier((got, *pieces))
    other = swap(got)
    grad_gate, mine = call(
        functools.partial(front_body, count, per, masks, *flips[:2]),
        (shape((channels, block_rows), BF16), shape((chips, 16, block_rows), BF16)),
        [pltpu.VMEM((features, 2 * block_rows), BF16), *wide],
        2 * features * channels * block_rows, got, other, *pieces, gate, conv,
    )
    cut = (3 * half + 15) // 16 * 8
    terms = shape((2, chips, cut, block_rows), BF16)
    keep, give = call(
        functools.partial(terms_body, count, masks, flips[2]),
        (terms, terms), [], 2 * features * channels * block_rows, *pieces, gate, conv,
    )
    opposite = lambda x: lax.ppermute(x, "seq", [(i, i ^ (count // 2)) for i in range(count)])
    part = shape((chips, cut, block_rows), BF16)
    summed, rest = call(join_body, (part, part), [], chips * (rows + half) * block_rows, keep, swap(give))
    mine = exchange(mine, flips[1])
    ordered = pltpu.VMEM((count * 8, block_rows), BF16)
    forms, tables = call(
        functools.partial(spectra_body, per, flips[0], channels),
        (shape((4, count * 8, block_rows), F32), shape((4, 2 * block_rows, block_rows), BF16)), [ordered],
        6 * count * 8 * block_rows * 2 * block_rows, got, other, window, forward, value_back, filter_back,
    )
    theirs = swap(mine)
    result = shape((chips, 16, block_rows), BF16)
    stay, leave = call(
        functools.partial(mix_body, count, *flips[1:]), (result, result),
        [
            ordered,
            pltpu.VMEM((count * 8, 2 * block_rows), F32),
            pltpu.VMEM((count * 8, 2 * block_rows), F32),
            pltpu.VMEM((count * 8 + 8, 2 * block_rows), F32),
        ],
        8 * count * 8 * block_rows * 2 * block_rows, mine, theirs, forms, tables,
    )
    both = call(
        last_body, shape((chips, 32 + cut, block_rows), BF16), [], 1000, stay, swap(leave), summed, opposite(rest)
    )
    grad_value, grad_filter, grad_weight = call(
        functools.partial(finish_body, per, flips[2]),
        (shape((channels, block_rows), BF16), shape((channels, block_rows), F32), shape((rows, channels), F32)),
        wide, 1000, exchange(both, flips[2]),
    )
    return (grad_value.T, grad_gate.T, grad_filter.T, grad_weight.T)


def solution(mesh):
    in_specs = (
        P("seq", "fsdp"),
        P("fsdp", "seq"),
        P("seq", "fsdp"),
        P("seq", "fsdp"),
        P("seq", "fsdp"),
        P("fsdp", None),
    )
    out_specs = (P("seq", "fsdp"), P("seq", "fsdp"), P("seq", "fsdp"), P("fsdp", "seq"))
    return jax.shard_map(body, mesh=mesh, in_specs=in_specs, out_specs=out_specs, check_vma=False)
```

```python
import functools

import jax
import jax.numpy as jnp
import numpy as np
from jax import lax
from jax.experimental import pallas as pl
from jax.experimental.pallas import tpu as pltpu
from jax.sharding import PartitionSpec as P

F32 = jnp.float32
BF16 = jnp.bfloat16


def make_tables(block_rows):
    n, period = block_rows, 2 * block_rows
    freq = np.arange(n)
    pos = np.arange(period)
    angle = 2.0 * np.pi * ((freq[:, None] * pos[None, :]) % period) / period
    cos = np.cos(angle)
    sin = np.sin(angle)
    sign = (1.0 - 2.0 * (freq % 2))[:, None]
    alt = (1.0 - 2.0 * (pos % 2))[None, :]
    narrow = lambda a: np.asarray(a, np.float32).astype(jnp.bfloat16)
    fwd_im = np.where(freq[:, None] == 0, alt, -sin)
    forward = np.concatenate([narrow(cos), narrow(fwd_im)], axis=0).T
    both = np.where(freq[:, None] == 0, 1.0, 2.0)
    back_cos = narrow(sign * cos / period).astype(np.float32) * both
    back_sin = narrow(-sign * sin / period).astype(np.float32) * both
    last = narrow(alt / period).astype(np.float32)
    first = freq[:, None] == 0
    value_back = np.concatenate([back_cos, np.where(first, last, -back_sin)], axis=0)[:, :n]
    filter_back = np.concatenate([back_cos, np.where(first, last, back_sin)], axis=0)
    return (
        np.ascontiguousarray(forward),
        np.ascontiguousarray(narrow(value_back)),
        np.ascontiguousarray(narrow(filter_back)),
    )


def dot(left, right, dims):
    return lax.dot_general(left, right, (dims, ((), ())), preferred_element_type=F32)


def call(body, out_shape, scratch, cost, *args, room=32 * 1024 * 1024, **specs):
    return pl.pallas_call(
        body,
        out_shape=out_shape,
        scratch_shapes=scratch,
        **specs,
        cost_estimate=pl.CostEstimate(flops=cost, bytes_accessed=1000000, transcendentals=0),
        compiler_params=pltpu.CompilerParams(vmem_limit_bytes=room),
    )(*args)


def window_start(per, length, size):
    return pl.multiple_of(jnp.minimum(lax.axis_index("seq") * per // 8 * 8, length - size), 8)


def pack_body(chips, per, flip, w_hbm, v_hbm, taps_ref, out_ref, window_ref, w_ref, v_ref, wide, sems):
    source = taps_ref.at[pl.ds(window_start(per, taps_ref.shape[0], window_ref.shape[0]), window_ref.shape[0])]
    pairs = ((w_hbm, w_ref), (v_hbm, v_ref), (source, window_ref))
    copies = [pltpu.make_async_copy(*pair, sems.at[i]) for i, pair in enumerate(pairs)]
    for copy in copies:
        copy.start()
    copies[0].wait()
    copies[1].wait()
    rows, channels = w_ref.shape
    half = rows // 2
    lanes = v_ref.shape[1]
    main = w_ref[:, :lanes]
    w = w_ref[...].astype(F32)
    side = jnp.concatenate([w[:half, lanes:], w[half:, lanes:]], axis=1).astype(BF16)
    wide[channels:, :] = jnp.zeros((wide.shape[0] - channels, lanes), F32)
    wide[:channels, :] = v_ref[...].astype(F32)
    for chip in range(chips):
        place = chip ^ flip
        out_ref[place, :rows, :] = main
        out_ref[place, rows : rows + half, :] = side
        for core in range(2):
            at = rows + half + 8 * core
            begin = per * (2 * chip + core)
            out_ref[place, at : at + 8, :] = wide[begin : begin + 8, :].astype(BF16)
    copies[2].wait()


def terms_body(groups, masks, flip, *refs):
    *pieces, g_ref, o_ref, keep_ref, send_ref = refs
    lanes = g_ref.shape[1]
    channels = g_ref.shape[0]
    here = lax.axis_index("fsdp")
    core = lax.rem(lax.axis_index("seq"), 2)
    late = lax.axis_index("seq") // (groups // 2)
    share = groups // len(masks)
    rows = channels // share
    half = rows // 2
    cut = keep_ref.shape[2]
    gated = (g_ref[...].astype(F32) * o_ref[...].astype(F32)).astype(BF16)
    rest = gated[lanes:]
    zero = jnp.zeros_like(rest)
    lower = jnp.concatenate([rest, zero], axis=0)
    upper = jnp.concatenate([zero, rest], axis=0)
    blocks = len(masks) // len(pieces)
    for part, source in enumerate(pieces):
        f = source[...].reshape(blocks * channels, lanes)
        main = dot(f, gated[:lanes], ((1,), (1,))).astype(BF16).reshape(blocks * share, rows, lanes)
        f3 = f.reshape(blocks * share, rows, lanes)
        low = f3[:, :half].reshape(blocks * share * half, lanes)
        high = f3[:, half:].reshape(blocks * share * half, lanes)
        side = dot(low, lower, ((1,), (1,))) + dot(high, upper, ((1,), (1,)))
        side = side.astype(BF16).reshape(blocks * share, half, lanes)

        def put(*refs):
            for i in range(blocks):
                first = jnp.bitwise_xor(here, masks[part * blocks + i]) * (share // 2)
                for q in range(share):
                    ref = refs[q % 2]
                    place = jnp.bitwise_xor(first + q // 2, flip)
                    ref[late, place] = main[i * share + q, :cut]
                    ref[1 - late, place, : rows - cut, :] = main[i * share + q, cut:]
                    ref[1 - late, place, rows - cut : rows - cut + half, :] = side[i * share + q]
                    ref[1 - late, place, rows - cut + half :, :] = jnp.zeros((2 * cut - rows - half, lanes), BF16)

        @pl.when(core == 0)
        def _():
            put(keep_ref, send_ref)

        @pl.when(core == 1)
        def _():
            put(send_ref, keep_ref)


def front_body(groups, per, masks, flip, flip_out, own_ref, other_ref, *refs):
    *pieces, g_ref, o_ref, gate_ref, out_ref, weight, wide = refs
    lanes = g_ref.shape[1]
    channels = g_ref.shape[0]
    here = lax.axis_index("fsdp")
    core = lax.rem(lax.axis_index("seq"), 2)
    share = groups // len(masks)
    rows = channels // share
    half = rows // 2
    for source, which in ((own_ref, core), (other_ref, 1 - core)):
        for slot in range(len(masks)):
            for q in range(share // 2):
                chip = jnp.bitwise_xor(jnp.bitwise_xor(here, masks[slot]) * (share // 2) + q, flip)
                at = pl.multiple_of(rows * (slot * share + 2 * q + which), 8)
                weight[pl.ds(at, rows), :lanes] = source[chip, :rows, :]
                side = source[chip, rows : rows + half, :]
                weight[pl.ds(at, half), lanes:] = side
                turned = jnp.concatenate([side[:, lanes // 2 :], side[:, : lanes // 2]], axis=1)
                weight[pl.ds(at + half, half), lanes:] = turned
    size = groups * rows // len(pieces)
    mixed = 0.0
    for part, source in enumerate(pieces):
        piece = weight[part * size : (part + 1) * size]
        mixed = mixed + dot(piece, source[...].reshape(size, lanes), ((0,), (0,)))
    mixed = mixed[:channels]
    gate_ref[...] = (mixed * o_ref[...].astype(F32)).astype(BF16)
    wide[channels:, :] = jnp.zeros((wide.shape[0] - channels, lanes), F32)
    wide[:channels, :] = mixed * g_ref[...].astype(F32)
    for chip in range(groups // 2):
        for c in range(2):
            begin = per * (2 * chip + c)
            out_ref[chip ^ flip_out, 8 * c : 8 * c + 8, :] = wide[begin : begin + 8, :].astype(BF16)


def in_order(own_ref, other_ref, row, flip, blocks):
    core = lax.rem(lax.axis_index("seq"), 2)
    at = pl.multiple_of(row + 8 * core, 8)
    for chip in range(own_ref.shape[0]):
        blocks[pl.ds(pl.multiple_of(16 * chip + 8 * core, 8), 8), :] = own_ref[chip ^ flip, pl.ds(at, 8), :]
        blocks[pl.ds(pl.multiple_of(16 * chip + 8 * (1 - core), 8), 8), :] = other_ref[chip ^ flip, pl.ds(at, 8), :]


def join_body(keep_ref, came_ref, stay_ref, leave_ref):
    stay_ref[...] = (keep_ref[0].astype(F32) + came_ref[0].astype(F32)).astype(BF16)
    leave_ref[...] = (keep_ref[1].astype(F32) + came_ref[1].astype(F32)).astype(BF16)


def spectra_body(
    per, flip, length, own_ref, other_ref, near_ref, table_ref, vback_ref, fback_ref, out_ref, tables_ref, blocks
):
    groups = 2 * own_ref.shape[0]
    lanes = own_ref.shape[2]
    window = near_ref.shape[0]
    start = lax.axis_index("seq") * per - window_start(per, length, window)
    rows = groups * 8
    table = table_ref[...]
    in_order(own_ref, other_ref, own_ref.shape[1] - 16, flip, blocks)
    val = dot(blocks[...], table[:lanes], ((1,), (0,)))
    out_ref[2] = val[:, :lanes]
    out_ref[3] = val[:, lanes:]
    own = pltpu.roll(near_ref[...].astype(F32), window - start, 0)[:8].astype(BF16)
    taps = jnp.concatenate([own[:, i * lanes : (i + 1) * lanes] for i in range(groups)], axis=0)
    upper = dot(taps, table[lanes:], ((1,), (0,)))
    lower = dot(taps, table[:lanes], ((1,), (0,)))
    lower = jnp.concatenate([jnp.zeros((8, 2 * lanes), F32), lower[: rows - 8]], axis=0)
    spec = upper + lower
    out_ref[0] = spec[:, :lanes]
    out_ref[1] = spec[:, lanes:]
    tables_ref[0, :lanes] = table[:lanes, :lanes]
    tables_ref[0, lanes:] = table[:lanes, lanes:]
    tables_ref[1] = vback_ref[...]
    tables_ref[2] = fback_ref[:, :lanes]
    tables_ref[3] = fback_ref[:, lanes:]


def mix_body(count, flip, flip_out, own_ref, other_ref, forms_ref, tables_ref, keep_ref, send_ref, blocks, conv, vmix, fmix):
    lanes = own_ref.shape[2]
    rows = count * 8
    in_order(own_ref, other_ref, 0, flip, blocks)
    g = blocks[...]
    conv[:, :lanes] = dot(g, tables_ref[0, :lanes], ((1,), (0,)))
    conv[:, lanes : 2 * lanes] = dot(g, tables_ref[0, lanes:], ((1,), (0,)))
    conv[:, 2 * lanes :] = conv[:, :lanes] + conv[:, lanes : 2 * lanes]
    first = lax.broadcasted_iota(jnp.int32, (8, lanes), 1) == 0
    tile = 8
    for base in range(0, count, tile):
        zero = jnp.zeros((8, lanes), F32)
        acc = [[zero] * 6 for _ in range(tile)]
        for shift in range(count - base):
            at = pl.ds(8 * shift, 8)
            tr, ti, vr, vi = (forms_ref[plane, at] for plane in range(4))
            tx, vx = ti - tr, vr - vi
            for r in range(min(tile, count - base - shift)):
                place = pl.ds(8 * (base + r + shift), 8)
                cr = conv[place, :lanes]
                ci = conv[place, lanes : 2 * lanes]
                cx = conv[place, 2 * lanes :]
                a = acc[r]
                acc[r] = [a[0] + cr * tr, a[1] + ci * ti, a[2] + cx * tx, a[3] + cr * vr, a[4] + ci * vi, a[5] + cx * vx]
        for r in range(tile):
            place = pl.ds(8 * (base + r), 8)
            a = acc[r]
            vmix[place, :lanes] = jnp.where(first, a[0], a[0] + a[1])
            vmix[place, lanes:] = jnp.where(first, a[1], a[2] + a[0] - a[1])
            fmix[place, :lanes] = jnp.where(first, a[3], a[3] + a[4])
            fmix[place, lanes:] = jnp.where(first, a[4], a[5] - a[3] + a[4])
    fmix[rows:, :] = jnp.zeros((8, 2 * lanes), F32)
    value = dot(vmix[...].astype(BF16), tables_ref[1], ((1,), (0,)))
    late = dot(fmix[:rows].astype(BF16), tables_ref[3], ((1,), (0,)))
    early = dot(fmix[8:].astype(BF16), tables_ref[2], ((1,), (0,)))
    value = value.astype(BF16).reshape(count, 8, lanes)
    lags = (late + early).astype(BF16).reshape(count, 8, lanes)

    def put(*refs):
        for i in range(count):
            refs[i % 2][(i // 2) ^ flip_out, :8, :] = value[i]
            refs[i % 2][(i // 2) ^ flip_out, 8:, :] = lags[i]

    core = lax.rem(lax.axis_index("seq"), 2)

    @pl.when(core == 0)
    def _():
        put(keep_ref, send_ref)

    @pl.when(core == 1)
    def _():
        put(send_ref, keep_ref)


def last_body(keep_ref, came_ref, terms_ref, more_ref, out_ref):
    core = lax.rem(lax.axis_index("seq"), 2)
    out_ref[:, pl.ds(pl.multiple_of(16 * core, 8), 16), :] = keep_ref[...]
    out_ref[:, pl.ds(pl.multiple_of(16 * (1 - core), 8), 16), :] = came_ref[...]
    out_ref[:, 32:, :] = (terms_ref[...].astype(F32) + more_ref[...].astype(F32)).astype(BF16)


def finish_body(per, flip, in_ref, value_ref, filter_ref, weight_ref, wide):
    chips, packed, lanes = in_ref.shape
    channels = value_ref.shape[0]
    for row, target in ((0, value_ref), (8, filter_ref)):
        for chip in range(chips):
            for c in range(2):
                at = per * (2 * chip + c)
                wide[at : at + 8, :] = in_ref[chip ^ flip, row + 16 * c : row + 16 * c + 8, :].astype(F32)
        target[...] = wide[:channels, :].astype(target.dtype)
    rows = weight_ref.shape[0]
    half = rows // 2
    first, second = in_ref[0 ^ flip, 32:, :].astype(F32), in_ref[(chips // 2) ^ flip, 32:, :].astype(F32)
    for chip in range(1, chips // 2):
        first = first + in_ref[chip ^ flip, 32:, :].astype(F32)
        second = second + in_ref[(chip + chips // 2) ^ flip, 32:, :].astype(F32)
    cut = packed - 32
    weight_ref[:cut, :lanes] = first
    weight_ref[cut:, :lanes] = second[: rows - cut]
    side = second[rows - cut : rows - cut + half]
    rest = channels - lanes
    weight_ref[:half, lanes:] = side[:, :rest]
    weight_ref[half:, lanes:] = side[:, rest:]


def body(cotangent, out_weight, values, gate_input, conv_out, filter_taps):
    block_rows, channels = values.shape
    count = lax.axis_size("seq")
    parts = lax.axis_size("fsdp")
    rows = out_weight.shape[1]
    features = rows * count
    per = channels // count
    forward, value_back, filter_back = (jnp.asarray(t) for t in make_tables(block_rows))
    cot, weight, vals = cotangent.T, out_weight.T, values.T
    gate, conv = gate_input.T, conv_out.T
    shape = jax.ShapeDtypeStruct
    chips = count // 2
    far_chip = chips // 2 + chips // 4
    flips = (far_chip, chips // 2, chips // 2)

    def exchange(x, flip):
        same_core = [[2 * (place ^ flip) + core for place in range(chips)] for core in range(2)]
        return lax.all_to_all(x, "seq", 0, 0, axis_index_groups=same_core)

    swap = lambda x: lax.ppermute(x, "seq", [(i, i ^ 1) for i in range(count)])
    cross = lambda x, mask: lax.ppermute(x, "fsdp", [(i, i ^ mask) for i in range(parts)])
    half = rows // 2
    wide = [pltpu.VMEM((channels + 8, block_rows), F32)]

    inside, outside = pl.BlockSpec(memory_space=pltpu.VMEM), pl.BlockSpec(memory_space=pltpu.HBM)
    sent, window = call(
        functools.partial(pack_body, chips, per, flips[0]),
        (shape((chips, rows + half + 16, block_rows), BF16), shape((16, filter_taps.shape[1]), BF16)),
        [pltpu.VMEM(weight.shape, BF16), pltpu.VMEM(vals.shape, BF16), *wide, pltpu.SemaphoreType.DMA((3,))],
        1000, weight, vals, filter_taps, room=60 * 1024 * 1024, in_specs=[outside] * 3, out_specs=(inside, inside),
    )
    across = cross(cot, parts // 2)
    sent, across = lax.optimization_barrier((sent, across))
    got = exchange(sent, flips[0])
    pair = jnp.stack([cot, across])
    pieces = [pair, cross(pair, 1), cross(pair, 3), cross(pair, 2)]
    masks = (0, 4, 1, 5, 3, 7, 2, 6)
    got, *pieces = lax.optimization_barrier((got, *pieces))
    other = swap(got)
    grad_gate, mine = call(
        functools.partial(front_body, count, per, masks, *flips[:2]),
        (shape((channels, block_rows), BF16), shape((chips, 16, block_rows), BF16)),
        [pltpu.VMEM((features, 2 * block_rows), BF16), *wide],
        2 * features * channels * block_rows, got, other, *pieces, gate, conv,
    )
    cut = (3 * half + 15) // 16 * 8
    terms = shape((2, chips, cut, block_rows), BF16)
    keep, give = call(
        functools.partial(terms_body, count, masks, flips[2]),
        (terms, terms), [], 2 * features * channels * block_rows, *pieces, gate, conv,
    )
    opposite = lambda x: lax.ppermute(x, "seq", [(i, i ^ (count // 2)) for i in range(count)])
    part = shape((chips, cut, block_rows), BF16)
    summed, rest = call(join_body, (part, part), [], chips * (rows + half) * block_rows, keep, swap(give))
    mine = exchange(mine, flips[1])
    ordered = pltpu.VMEM((count * 8, block_rows), BF16)
    forms, tables = call(
        functools.partial(spectra_body, per, flips[0], channels),
        (shape((4, count * 8, block_rows), F32), shape((4, 2 * block_rows, block_rows), BF16)), [ordered],
        6 * count * 8 * block_rows * 2 * block_rows, got, other, window, forward, value_back, filter_back,
    )
    theirs = swap(mine)
    result = shape((chips, 16, block_rows), BF16)
    stay, leave = call(
        functools.partial(mix_body, count, *flips[1:]), (result, result),
        [
            ordered,
            pltpu.VMEM((count * 8, 3 * block_rows), F32),
            pltpu.VMEM((count * 8, 2 * block_rows), F32),
            pltpu.VMEM((count * 8 + 8, 2 * block_rows), F32),
        ],
        8 * count * 8 * block_rows * 2 * block_rows, mine, theirs, forms, tables,
    )
    both = call(
        last_body, shape((chips, 32 + cut, block_rows), BF16), [], 1000, stay, swap(leave), summed, opposite(rest)
    )
    grad_value, grad_filter, grad_weight = call(
        functools.partial(finish_body, per, flips[2]),
        (shape((channels, block_rows), BF16), shape((channels, block_rows), F32), shape((rows, channels), F32)),
        wide, 1000, exchange(both, flips[2]),
    )
    return (grad_value.T, grad_gate.T, grad_filter.T, grad_weight.T)


def solution(mesh):
    in_specs = (
        P("seq", "fsdp"),
        P("fsdp", "seq"),
        P("seq", "fsdp"),
        P("seq", "fsdp"),
        P("seq", "fsdp"),
        P("fsdp", None),
    )
    out_specs = (P("seq", "fsdp"), P("seq", "fsdp"), P("seq", "fsdp"), P("fsdp", "seq"))
    return jax.shard_map(body, mesh=mesh, in_specs=in_specs, out_specs=out_specs, check_vma=False)
```

```python
import functools

import jax
import jax.numpy as jnp
import numpy as np
from jax import lax
from jax.experimental import pallas as pl
from jax.experimental.pallas import tpu as pltpu
from jax.sharding import PartitionSpec as P

F32 = jnp.float32
BF16 = jnp.bfloat16


def make_tables(block_rows):
    n, period = block_rows, 2 * block_rows
    freq = np.arange(n)
    pos = np.arange(period)
    angle = 2.0 * np.pi * ((freq[:, None] * pos[None, :]) % period) / period
    cos = np.cos(angle)
    sin = np.sin(angle)
    sign = (1.0 - 2.0 * (freq % 2))[:, None]
    alt = (1.0 - 2.0 * (pos % 2))[None, :]
    narrow = lambda a: np.asarray(a, np.float32).astype(jnp.bfloat16)
    fwd_im = np.where(freq[:, None] == 0, alt, -sin)
    forward = np.concatenate([narrow(cos), narrow(fwd_im)], axis=0).T
    both = np.where(freq[:, None] == 0, 1.0, 2.0)
    back_cos = narrow(sign * cos / period).astype(np.float32) * both
    back_sin = narrow(-sign * sin / period).astype(np.float32) * both
    last = narrow(alt / period).astype(np.float32)
    first = freq[:, None] == 0
    value_back = np.concatenate([back_cos, np.where(first, last, -back_sin)], axis=0)[:, :n]
    filter_back = np.concatenate([back_cos, np.where(first, last, back_sin)], axis=0)
    return (
        np.ascontiguousarray(forward),
        np.ascontiguousarray(narrow(value_back)),
        np.ascontiguousarray(narrow(filter_back)),
    )


def dot(left, right, dims):
    return lax.dot_general(left, right, (dims, ((), ())), preferred_element_type=F32)


def call(body, out_shape, scratch, cost, *args, room=32 * 1024 * 1024, **specs):
    return pl.pallas_call(
        body,
        out_shape=out_shape,
        scratch_shapes=scratch,
        **specs,
        cost_estimate=pl.CostEstimate(flops=cost, bytes_accessed=1000000, transcendentals=0),
        compiler_params=pltpu.CompilerParams(vmem_limit_bytes=room),
    )(*args)


def window_start(per, length, size):
    return pl.multiple_of(jnp.minimum(lax.axis_index("seq") * per // 8 * 8, length - size), 8)


def pack_body(chips, per, flip, w_hbm, v_hbm, taps_ref, out_ref, window_ref, w_ref, v_ref, wide, sems):
    source = taps_ref.at[pl.ds(window_start(per, taps_ref.shape[0], window_ref.shape[0]), window_ref.shape[0])]
    pairs = ((w_hbm, w_ref), (v_hbm, v_ref), (source, window_ref))
    copies = [pltpu.make_async_copy(*pair, sems.at[i]) for i, pair in enumerate(pairs)]
    for copy in copies:
        copy.start()
    copies[0].wait()
    copies[1].wait()
    rows, channels = w_ref.shape
    half = rows // 2
    lanes = v_ref.shape[1]
    main = w_ref[:, :lanes]
    w = w_ref[...].astype(F32)
    side = jnp.concatenate([w[:half, lanes:], w[half:, lanes:]], axis=1).astype(BF16)
    wide[channels:, :] = jnp.zeros((wide.shape[0] - channels, lanes), F32)
    wide[:channels, :] = v_ref[...].astype(F32)
    for chip in range(chips):
        place = chip ^ flip
        out_ref[place, :rows, :] = main
        out_ref[place, rows : rows + half, :] = side
        for core in range(2):
            at = rows + half + 8 * core
            begin = per * (2 * chip + core)
            out_ref[place, at : at + 8, :] = wide[begin : begin + 8, :].astype(BF16)
    copies[2].wait()


def terms_body(groups, masks, flip, *refs):
    *pieces, g_ref, o_ref, keep_ref, send_ref = refs
    lanes = g_ref.shape[1]
    channels = g_ref.shape[0]
    here = lax.axis_index("fsdp")
    core = lax.rem(lax.axis_index("seq"), 2)
    late = lax.axis_index("seq") // (groups // 2)
    share = groups // len(masks)
    rows = channels // share
    half = rows // 2
    cut = keep_ref.shape[2]
    gated = (g_ref[...].astype(F32) * o_ref[...].astype(F32)).astype(BF16)
    rest = gated[lanes:]
    zero = jnp.zeros_like(rest)
    lower = jnp.concatenate([rest, zero], axis=0)
    upper = jnp.concatenate([zero, rest], axis=0)
    blocks = len(masks) // len(pieces)
    for part, source in enumerate(pieces):
        f = source[...].reshape(blocks * channels, lanes)
        main = dot(f, gated[:lanes], ((1,), (1,))).astype(BF16).reshape(blocks * share, rows, lanes)
        f3 = f.reshape(blocks * share, rows, lanes)
        low = f3[:, :half].reshape(blocks * share * half, lanes)
        high = f3[:, half:].reshape(blocks * share * half, lanes)
        side = dot(low, lower, ((1,), (1,))) + dot(high, upper, ((1,), (1,)))
        side = side.astype(BF16).reshape(blocks * share, half, lanes)

        def put(*refs):
            for i in range(blocks):
                first = jnp.bitwise_xor(here, masks[part * blocks + i]) * (share // 2)
                for q in range(share):
                    ref = refs[q % 2]
                    place = jnp.bitwise_xor(first + q // 2, flip)
                    ref[late, place] = main[i * share + q, :cut]
                    ref[1 - late, place, : rows - cut, :] = main[i * share + q, cut:]
                    ref[1 - late, place, rows - cut : rows - cut + half, :] = side[i * share + q]
                    ref[1 - late, place, rows - cut + half :, :] = jnp.zeros((2 * cut - rows - half, lanes), BF16)

        @pl.when(core == 0)
        def _():
            put(keep_ref, send_ref)

        @pl.when(core == 1)
        def _():
            put(send_ref, keep_ref)


def front_body(groups, per, masks, flip, flip_out, own_ref, other_ref, *refs):
    *pieces, g_ref, o_ref, gate_ref, out_ref, weight, wide = refs
    lanes = g_ref.shape[1]
    channels = g_ref.shape[0]
    here = lax.axis_index("fsdp")
    core = lax.rem(lax.axis_index("seq"), 2)
    share = groups // len(masks)
    rows = channels // share
    half = rows // 2
    for source, which in ((own_ref, core), (other_ref, 1 - core)):
        for slot in range(len(masks)):
            for q in range(share // 2):
                chip = jnp.bitwise_xor(jnp.bitwise_xor(here, masks[slot]) * (share // 2) + q, flip)
                at = pl.multiple_of(rows * (slot * share + 2 * q + which), 8)
                weight[pl.ds(at, rows), :lanes] = source[chip, :rows, :]
                side = source[chip, rows : rows + half, :]
                weight[pl.ds(at, half), lanes:] = side
                turned = jnp.concatenate([side[:, lanes // 2 :], side[:, : lanes // 2]], axis=1)
                weight[pl.ds(at + half, half), lanes:] = turned
    size = groups * rows // len(pieces)
    mixed = 0.0
    for part, source in enumerate(pieces):
        piece = weight[part * size : (part + 1) * size]
        mixed = mixed + dot(piece, source[...].reshape(size, lanes), ((0,), (0,)))
    mixed = mixed[:channels]
    gate_ref[...] = (mixed * o_ref[...].astype(F32)).astype(BF16)
    wide[channels:, :] = jnp.zeros((wide.shape[0] - channels, lanes), F32)
    wide[:channels, :] = mixed * g_ref[...].astype(F32)
    for chip in range(groups // 2):
        for c in range(2):
            begin = per * (2 * chip + c)
            out_ref[chip ^ flip_out, 8 * c : 8 * c + 8, :] = wide[begin : begin + 8, :].astype(BF16)


def in_order(own_ref, other_ref, row, flip, blocks):
    core = lax.rem(lax.axis_index("seq"), 2)
    at = pl.multiple_of(row + 8 * core, 8)
    for chip in range(own_ref.shape[0]):
        blocks[pl.ds(pl.multiple_of(16 * chip + 8 * core, 8), 8), :] = own_ref[chip ^ flip, pl.ds(at, 8), :]
        blocks[pl.ds(pl.multiple_of(16 * chip + 8 * (1 - core), 8), 8), :] = other_ref[chip ^ flip, pl.ds(at, 8), :]


def join_body(keep_ref, came_ref, stay_ref, leave_ref):
    stay_ref[...] = (keep_ref[0].astype(F32) + came_ref[0].astype(F32)).astype(BF16)
    leave_ref[...] = (keep_ref[1].astype(F32) + came_ref[1].astype(F32)).astype(BF16)


def spectra_body(
    per, flip, length, own_ref, other_ref, near_ref, table_ref, vback_ref, fback_ref, out_ref, tables_ref, blocks
):
    groups = 2 * own_ref.shape[0]
    lanes = own_ref.shape[2]
    window = near_ref.shape[0]
    start = lax.axis_index("seq") * per - window_start(per, length, window)
    rows = groups * 8
    table = table_ref[...]
    in_order(own_ref, other_ref, own_ref.shape[1] - 16, flip, blocks)
    val = dot(blocks[...], table[:lanes], ((1,), (0,)))
    out_ref[2] = val[:, :lanes]
    out_ref[3] = val[:, lanes:]
    own = pltpu.roll(near_ref[...].astype(F32), window - start, 0)[:8].astype(BF16)
    taps = jnp.concatenate([own[:, i * lanes : (i + 1) * lanes] for i in range(groups)], axis=0)
    upper = dot(taps, table[lanes:], ((1,), (0,)))
    lower = dot(taps, table[:lanes], ((1,), (0,)))
    lower = jnp.concatenate([jnp.zeros((8, 2 * lanes), F32), lower[: rows - 8]], axis=0)
    spec = upper + lower
    out_ref[0] = spec[:, :lanes]
    out_ref[1] = spec[:, lanes:]
    tables_ref[0, :lanes] = table[:lanes, :lanes]
    tables_ref[0, lanes:] = table[:lanes, lanes:]
    tables_ref[1] = vback_ref[...]
    tables_ref[2] = fback_ref[:, :lanes]
    tables_ref[3] = fback_ref[:, lanes:]


def mix_body(count, flip, flip_out, own_ref, other_ref, forms_ref, tables_ref, keep_ref, send_ref, blocks, conv, vmix, fmix):
    lanes = own_ref.shape[2]
    rows = count * 8
    in_order(own_ref, other_ref, 0, flip, blocks)
    g = blocks[...]
    conv[:, :lanes] = dot(g, tables_ref[0, :lanes], ((1,), (0,)))
    conv[:, lanes : 2 * lanes] = dot(g, tables_ref[0, lanes:], ((1,), (0,)))
    conv[:, 2 * lanes :] = conv[:, :lanes] + conv[:, lanes : 2 * lanes]
    first = lax.broadcasted_iota(jnp.int32, (8, lanes), 1) == 0
    tile = 8
    for base in range(0, count, tile):
        zero = jnp.zeros((8, lanes), F32)
        acc = [[zero] * 6 for _ in range(tile)]
        for shift in range(count - base):
            at = pl.ds(8 * shift, 8)
            tr, ti, vr, vi = (forms_ref[plane, at] for plane in range(4))
            tx, vx = ti - tr, vr - vi
            for r in range(min(tile, count - base - shift)):
                place = pl.ds(8 * (base + r + shift), 8)
                cr = conv[place, :lanes]
                ci = conv[place, lanes : 2 * lanes]
                cx = conv[place, 2 * lanes :]
                a = acc[r]
                acc[r] = [a[0] + cr * tr, a[1] + ci * ti, a[2] + cx * tx, a[3] + cr * vr, a[4] + ci * vi, a[5] + cx * vx]
        for r in range(tile):
            place = pl.ds(8 * (base + r), 8)
            a = acc[r]
            vmix[place, :lanes] = jnp.where(first, a[0], a[0] + a[1])
            vmix[place, lanes:] = jnp.where(first, a[1], a[2] + a[0] - a[1])
            fmix[place, :lanes] = jnp.where(first, a[3], a[3] + a[4])
            fmix[place, lanes:] = jnp.where(first, a[4], a[5] - a[3] + a[4])
    fmix[rows:, :] = jnp.zeros((8, 2 * lanes), F32)
    value = dot(vmix[...].astype(BF16), tables_ref[1], ((1,), (0,)))
    late = dot(fmix[:rows].astype(BF16), tables_ref[3], ((1,), (0,)))
    early = dot(fmix[8:].astype(BF16), tables_ref[2], ((1,), (0,)))
    value = value.astype(BF16).reshape(count, 8, lanes)
    lags = (late + early).astype(BF16).reshape(count, 8, lanes)

    def put(*refs):
        for i in range(count):
            refs[i % 2][(i // 2) ^ flip_out, :8, :] = value[i]
            refs[i % 2][(i // 2) ^ flip_out, 8:, :] = lags[i]

    core = lax.rem(lax.axis_index("seq"), 2)

    @pl.when(core == 0)
    def _():
        put(keep_ref, send_ref)

    @pl.when(core == 1)
    def _():
        put(send_ref, keep_ref)


def last_body(per, keep_ref, came_ref, terms_ref, more_ref, out_ref, tight):
    core = lax.rem(lax.axis_index("seq"), 2)
    keep, came = keep_ref[...].astype(F32), came_ref[...].astype(F32)
    for c in range(2):
        rows = jnp.where(core == c, keep, came)
        tight[:, 2 * per * c : 2 * per * c + 8, :] = rows[:, :8]
        tight[:, 2 * per * c + per : 2 * per * c + per + 8, :] = rows[:, 8:]
    out_ref[:, : 4 * per, :] = tight[:, : 4 * per, :].astype(BF16)
    out_ref[:, 4 * per :, :] = (terms_ref[...].astype(F32) + more_ref[...].astype(F32)).astype(BF16)


def finish_body(per, flip, in_ref, value_ref, filter_ref, weight_ref, wide, tight):
    chips, packed, lanes = in_ref.shape
    channels = value_ref.shape[0]
    tight[:, : 4 * per, :] = in_ref[:, : 4 * per, :].astype(F32)
    tight[:, 4 * per :, :] = jnp.zeros((chips, tight.shape[1] - 4 * per, lanes), F32)
    for row, target in ((0, value_ref), (per, filter_ref)):
        for chip in range(chips):
            for c in range(2):
                at, begin = per * (2 * chip + c), row + 2 * per * c
                wide[at : at + 8, :] = tight[chip ^ flip, begin : begin + 8, :]
        target[...] = wide[:channels, :].astype(target.dtype)
    rows = weight_ref.shape[0]
    half = rows // 2
    head = 4 * per
    first, second = in_ref[0 ^ flip, head:, :].astype(F32), in_ref[(chips // 2) ^ flip, head:, :].astype(F32)
    for chip in range(1, chips // 2):
        first = first + in_ref[chip ^ flip, head:, :].astype(F32)
        second = second + in_ref[(chip + chips // 2) ^ flip, head:, :].astype(F32)
    cut = packed - head
    weight_ref[:cut, :lanes] = first
    weight_ref[cut:, :lanes] = second[: rows - cut]
    side = second[rows - cut : rows - cut + half]
    rest = channels - lanes
    weight_ref[:half, lanes:] = side[:, :rest]
    weight_ref[half:, lanes:] = side[:, rest:]


def body(cotangent, out_weight, values, gate_input, conv_out, filter_taps):
    block_rows, channels = values.shape
    count = lax.axis_size("seq")
    parts = lax.axis_size("fsdp")
    rows = out_weight.shape[1]
    features = rows * count
    per = channels // count
    forward, value_back, filter_back = (jnp.asarray(t) for t in make_tables(block_rows))
    cot, weight, vals = cotangent.T, out_weight.T, values.T
    gate, conv = gate_input.T, conv_out.T
    shape = jax.ShapeDtypeStruct
    chips = count // 2
    far_chip = chips // 2 + chips // 4
    flips = (far_chip, chips // 2, chips // 2)

    def exchange(x, flip):
        same_core = [[2 * (place ^ flip) + core for place in range(chips)] for core in range(2)]
        return lax.all_to_all(x, "seq", 0, 0, axis_index_groups=same_core)

    swap = lambda x: lax.ppermute(x, "seq", [(i, i ^ 1) for i in range(count)])
    cross = lambda x, mask: lax.ppermute(x, "fsdp", [(i, i ^ mask) for i in range(parts)])
    half = rows // 2
    wide = [pltpu.VMEM((channels + 8, block_rows), F32)]

    inside, outside = pl.BlockSpec(memory_space=pltpu.VMEM), pl.BlockSpec(memory_space=pltpu.HBM)
    sent, window = call(
        functools.partial(pack_body, chips, per, flips[0]),
        (shape((chips, rows + half + 16, block_rows), BF16), shape((16, filter_taps.shape[1]), BF16)),
        [pltpu.VMEM(weight.shape, BF16), pltpu.VMEM(vals.shape, BF16), *wide, pltpu.SemaphoreType.DMA((3,))],
        1000, weight, vals, filter_taps, room=60 * 1024 * 1024, in_specs=[outside] * 3, out_specs=(inside, inside),
    )
    across = cross(cot, parts // 2)
    sent, across = lax.optimization_barrier((sent, across))
    got = exchange(sent, flips[0])
    pair = jnp.stack([cot, across])
    pieces = [pair, cross(pair, 1), cross(pair, 3), cross(pair, 2)]
    masks = (0, 4, 1, 5, 3, 7, 2, 6)
    got, *pieces = lax.optimization_barrier((got, *pieces))
    other = swap(got)
    grad_gate, mine = call(
        functools.partial(front_body, count, per, masks, *flips[:2]),
        (shape((channels, block_rows), BF16), shape((chips, 16, block_rows), BF16)),
        [pltpu.VMEM((features, 2 * block_rows), BF16), *wide],
        2 * features * channels * block_rows, got, other, *pieces, gate, conv,
    )
    cut = (3 * half + 15) // 16 * 8
    terms = shape((2, chips, cut, block_rows), BF16)
    keep, give = call(
        functools.partial(terms_body, count, masks, flips[2]),
        (terms, terms), [], 2 * features * channels * block_rows, *pieces, gate, conv,
    )
    opposite = lambda x: lax.ppermute(x, "seq", [(i, i ^ (count // 2)) for i in range(count)])
    part = shape((chips, cut, block_rows), BF16)
    summed, rest = call(join_body, (part, part), [], chips * (rows + half) * block_rows, keep, swap(give))
    mine = exchange(mine, flips[1])
    ordered = pltpu.VMEM((count * 8, block_rows), BF16)
    forms, tables = call(
        functools.partial(spectra_body, per, flips[0], channels),
        (shape((4, count * 8, block_rows), F32), shape((4, 2 * block_rows, block_rows), BF16)), [ordered],
        6 * count * 8 * block_rows * 2 * block_rows, got, other, window, forward, value_back, filter_back,
    )
    theirs = swap(mine)
    result = shape((chips, 16, block_rows), BF16)
    stay, leave = call(
        functools.partial(mix_body, count, *flips[1:]), (result, result),
        [
            ordered,
            pltpu.VMEM((count * 8, 3 * block_rows), F32),
            pltpu.VMEM((count * 8, 2 * block_rows), F32),
            pltpu.VMEM((count * 8 + 8, 2 * block_rows), F32),
        ],
        8 * count * 8 * block_rows * 2 * block_rows, mine, theirs, forms, tables,
    )
    tight = pltpu.VMEM((chips, 4 * per + 8, block_rows), F32)
    both = call(
        functools.partial(last_body, per), shape((chips, 4 * per + cut, block_rows), BF16), [tight], 1000,
        stay, swap(leave), summed, opposite(rest)
    )
    grad_value, grad_filter, grad_weight = call(
        functools.partial(finish_body, per, flips[2]),
        (shape((channels, block_rows), BF16), shape((channels, block_rows), F32), shape((rows, channels), F32)),
        [*wide, tight], 1000, exchange(both, flips[2]),
    )
    return (grad_value.T, grad_gate.T, grad_filter.T, grad_weight.T)


def solution(mesh):
    in_specs = (
        P("seq", "fsdp"),
        P("fsdp", "seq"),
        P("seq", "fsdp"),
        P("seq", "fsdp"),
        P("seq", "fsdp"),
        P("fsdp", None),
    )
    out_specs = (P("seq", "fsdp"), P("seq", "fsdp"), P("seq", "fsdp"), P("fsdp", "seq"))
    return jax.shard_map(body, mesh=mesh, in_specs=in_specs, out_specs=out_specs, check_vma=False)
```
